32 devices in a mesh: dp: 16 (over z, x, core), tensor: 2 (over y).
Axes of the slice: x: 2, y: 2, z: 4, core: 2. Of those that a mesh axis runs over, the one named last changes fastest.
Arguments:
- tokens: bfloat16 [4096, 1024], P(('dp', 'tensor')), may hold values from -6 to 6
- seq_lens: int32 [16, 8], P('dp'), may hold values from 0 to 256, as said below
- g_attn: bfloat16 [1024], P('dp'), may hold values from 0.5 to 1.5
- w_qkv: bfloat16 [1024, 3, 1024], P('dp', None, 'tensor'), may hold values from -0.1875 to 0.1875
- w_ao: bfloat16 [1024, 1024], P('tensor', 'dp'), may hold values from -0.75 to 0.75
- g_mlp: bfloat16 [1024], P('dp'), may hold values from 0.5 to 1.5
- w_in: bfloat16 [1024, 2, 2624], P('dp', None, 'tensor'), may hold values from -0.1875 to 0.1875
- w_mo: bfloat16 [2624, 1024], P('tensor', 'dp'), may hold values from -0.15625 to 0.15625
- cotangent: bfloat16 [4096, 1024], P(('dp', 'tensor')), may hold values from -6 to 6
Outputs:
- output: bfloat16 [4096, 1024], P(('dp', 'tensor'))
- grad_input: float32 [4096, 1024], P(('dp', 'tensor'))
- grad_g_attn: float32 [1024], P(('dp', 'tensor'))
- grad_qkv: float32 [1024, 3, 1024], P('dp', None, 'tensor')
- grad_ao: float32 [1024, 1024], P('tensor', 'dp')
- grad_g_mlp: float32 [1024], P(('dp', 'tensor'))
- grad_in: float32 [1024, 2, 2624], P('dp', None, 'tensor')
- grad_mo: float32 [2624, 1024], P('tensor', 'dp')
The draws below stay inside these ranges and needn't reach their ends.
Inputs may be any that keep to these rules, and one draw needn't show every extreme that they name: `seq_lens`: A group's lengths sum to at most 256; a length of 0 is an empty slot; in every draw some group holds one sequence of 256 tokens.
All inputs are finite; a program needn't handle non-finite values.
Results may differ from the reference program's by a relative error of at most 0.014.
Values may be sent and summed in bfloat16 or wider, within the bound.
No kernel may reach another device: no remote copies, remote signals or barrier semaphores. Data moves between devices by JAX's collectives and lax.ppermute only.
A program may use at most 128 MiB of HBM per device.

```python
import math
import jax
import jax.numpy as jnp
from jax import lax

D = 1024
HEADS = 16
HDIM = 64
FF = 2624
CAP = 256
SEQS = 8
TOKENS = 4096
N_DP = 16


def draw_seq_lens(key, part):
    key_fill = jax.random.fold_in(key, 11)
    key_full = jax.random.fold_in(key, 12)
    key_cuts = jax.random.fold_in(key, 13)
    groups = jnp.arange(N_DP, dtype=jnp.int32)
    filled = jax.random.randint(key_fill, (N_DP,), CAP // 4, CAP + 1).astype(jnp.int32)
    chosen = jax.random.randint(key_full, (), 0, N_DP).astype(jnp.int32)
    filled = jnp.where(groups == chosen, CAP, filled).astype(jnp.int32)
    cuts = jax.random.randint(key_cuts, (N_DP, SEQS - 1), 0, filled[:, None] + 1).astype(jnp.int32)
    cuts = jnp.where((groups == chosen)[:, None], 0, cuts).astype(jnp.int32)
    cuts = jnp.sort(cuts, axis=1)
    edges = jnp.concatenate([jnp.zeros((N_DP, 1), jnp.int32), cuts, filled[:, None]], axis=1)
    return (edges[:, 1:] - edges[:, :-1]).astype(jnp.int32)


def block_scale(stream_key, extent, pieces, low, high):
    level = 1.0
    for axis_at, shards_of in pieces:
        draws = jax.random.uniform(jax.random.fold_in(jax.random.fold_in(stream_key, 6), axis_at), (shards_of,), jnp.float32, low / len(pieces), high / len(pieces))
        level = level * jnp.repeat(jnp.exp(draws), extent[axis_at] // shards_of).reshape((-1,) + (1,) * (len(extent) - 1 - axis_at))
    return level


def normal_values(rng, dims, scale, reach, pieces=(), kind=jnp.bfloat16):
    array = scale * jax.random.normal(rng, dims, jnp.float32)
    if pieces:
        array = array * block_scale(rng, dims, pieces, -0.22, 0.18)
    return jnp.clip(array, -reach, reach).astype(kind)


def setup_inputs(seed: int = 0) -> dict:
    keys = jax.random.split(jax.random.key(seed), 10)
    return {
        "tokens": normal_values(keys[0], (TOKENS, D), 1.0, 6.0, ((0, 32),)),
        "seq_lens": draw_seq_lens(jax.random.fold_in(keys[9], 71), 0),
        "g_attn": jnp.clip(1.0 + 0.1 * jax.random.normal(keys[2], (D,), jnp.float32), 0.5, 1.5).astype(jnp.bfloat16),
        "w_qkv": normal_values(keys[3], (D, 3, D), D ** -0.5, 0.1875, ((0, 16), (2, 2))),
        "w_ao": normal_values(keys[4], (D, D), (D // 16) ** -0.5, 0.75, ((0, 2), (1, 16))),
        "g_mlp": jnp.clip(1.0 + 0.1 * jax.random.normal(keys[5], (D,), jnp.float32), 0.5, 1.5).astype(jnp.bfloat16),
        "w_in": normal_values(keys[6], (D, 2, FF), D ** -0.5, 0.1875, ((0, 16), (2, 2))),
        "w_mo": normal_values(keys[7], (FF, D), (FF // 2) ** -0.5, 0.15625, ((0, 2), (1, 16))),
        "cotangent": normal_values(keys[8], (TOKENS, D), 1.0, 6.0, ((0, 32),)),
    }


ROPE_BASE = 160000.0

def layout(lengths, count):
    ends = jnp.cumsum(lengths).astype(jnp.int32)
    index = jnp.arange(count, dtype=jnp.int32)
    passed = ends[None, :] <= index[:, None]
    doc_ids = lax.optimization_barrier(jnp.sum(passed.astype(jnp.int32), axis=1)).astype(jnp.int32)
    begins = lax.optimization_barrier(jnp.max(jnp.where(passed, ends[None, :], jnp.zeros_like(ends)[None, :]), axis=1)).astype(jnp.int32)
    return (doc_ids, (index - begins).astype(jnp.int32))

def tables(positions):
    half = HDIM // 2
    rates = jnp.exp(jnp.arange(half, dtype=jnp.float32) * (-2.0 * math.log(ROPE_BASE) / HDIM))
    angles = positions.astype(jnp.float32)[:, None] * rates[None, :]
    return (jnp.cos(angles)[:, None, :], jnp.sin(angles)[:, None, :])

def rotate(values, cosine, sine):
    half = values.shape[-1] // 2
    first = values[..., :half]
    second = values[..., half:]
    return jnp.concatenate([first * cosine - second * sine, second * cosine + first * sine], axis=-1)

def unrotate(grads, cosine, sine):
    half = grads.shape[-1] // 2
    first = grads[..., :half]
    second = grads[..., half:]
    return jnp.concatenate([first * cosine + second * sine, second * cosine - first * sine], axis=-1)

def normalize(values):
    center = values - lax.optimization_barrier(jnp.mean(values, axis=-1, keepdims=True))
    factor = lax.rsqrt(lax.optimization_barrier(jnp.mean(center * center, axis=-1, keepdims=True)) + 1e-05)
    return (center * factor, factor)

def norm_back(grad_norm, gain, normed, factor):
    grad_hat = grad_norm * gain
    return factor * (grad_hat - lax.optimization_barrier(jnp.mean(grad_hat, axis=-1, keepdims=True)) - normed * lax.optimization_barrier(jnp.mean(grad_hat * normed, axis=-1, keepdims=True)))

def gelu_exact(values):
    return jax.nn.gelu(values, approximate=False)

def fdot(left, right):
    return jnp.dot(left, right, preferred_element_type=jnp.float32)

def scores_of(queries, key_rows, same_doc):
    raw = jnp.einsum('qhd,khd->hqk', queries.astype(jnp.float32), key_rows.astype(jnp.float32)) * 0.125
    return jnp.where(same_doc[None], raw, -1e+30)

def attend(queries, key_rows, values, same_doc):
    scores = scores_of(queries, key_rows, same_doc)
    peak = lax.optimization_barrier(jnp.max(scores, axis=-1, keepdims=True))
    log_total = peak + jnp.log(lax.optimization_barrier(jnp.sum(jnp.exp(scores - peak), axis=-1, keepdims=True)))
    weights = jnp.exp(scores - log_total).astype(jnp.bfloat16)
    mixed = jnp.einsum('hqk,khd->qhd', weights.astype(jnp.float32), values.astype(jnp.float32))
    return (mixed.astype(jnp.bfloat16), log_total)

def attend_back(queries, key_rows, values, same_doc, log_total, grad_out):
    probs = jnp.exp(scores_of(queries, key_rows, same_doc) - log_total)
    rounded = probs.astype(jnp.bfloat16).astype(jnp.float32)
    grad_wide = grad_out.astype(jnp.float32)
    grad_values = jnp.einsum('hqk,qhd->khd', rounded, grad_wide)
    grad_probs = jnp.einsum('qhd,khd->hqk', grad_wide, values.astype(jnp.float32))
    inner = lax.optimization_barrier(jnp.sum(probs * grad_probs, axis=-1, keepdims=True))
    grad_scores = (probs * (grad_probs - inner) * 0.125).astype(jnp.bfloat16).astype(jnp.float32)
    grad_queries = jnp.einsum('hqk,khd->qhd', grad_scores, key_rows.astype(jnp.float32))
    grad_keys = jnp.einsum('hqk,qhd->khd', grad_scores, queries.astype(jnp.float32))
    return (grad_queries, grad_keys, grad_values)

def group_pass(weights, block, cot_block, lengths):
    gain_one, full_qkv, full_ao, gain_two, full_in, full_mo = weights
    group = block.shape[0]
    doc_ids, positions = layout(lengths, group)
    same_doc = doc_ids[:, None] == doc_ids[None, :]
    cosine, sine = tables(positions)
    head_shape = (group, HEADS, HDIM)
    inputs = block.astype(jnp.float32)
    normed_one, factor_one = normalize(inputs)
    ln_one = (normed_one * gain_one).astype(jnp.bfloat16)
    projected = jnp.einsum('td,dcn->tcn', ln_one.astype(jnp.float32), full_qkv.astype(jnp.float32))
    queries = rotate(projected[:, 0].reshape(head_shape), cosine, sine).astype(jnp.bfloat16)
    key_rows = rotate(projected[:, 1].reshape(head_shape), cosine, sine).astype(jnp.bfloat16)
    values = projected[:, 2].reshape(head_shape).astype(jnp.bfloat16)
    mixed, log_total = attend(queries, key_rows, values, same_doc)
    flat_mixed = mixed.reshape(group, -1)
    residual = inputs + fdot(flat_mixed, full_ao)
    normed_two, factor_two = normalize(residual)
    ln_two = (normed_two * gain_two).astype(jnp.bfloat16)
    gate_up = jnp.einsum('td,dcn->tcn', ln_two.astype(jnp.float32), full_in.astype(jnp.float32))
    gate = gate_up[:, 0]
    upper = gate_up[:, 1]
    product = (gelu_exact(gate) * upper).astype(jnp.bfloat16)
    output = (residual + fdot(product, full_mo)).astype(jnp.bfloat16)
    grad_mo = fdot(product.T, cot_block)
    grad_product = fdot(cot_block, full_mo.T)
    activated, pull = jax.vjp(gelu_exact, gate)
    grad_gate = pull(grad_product * upper)[0]
    grad_gate_up = jnp.stack([grad_gate, grad_product * activated], axis=1).astype(jnp.bfloat16).astype(jnp.float32)
    grad_in = jnp.einsum('td,tcn->dcn', ln_two.astype(jnp.float32), grad_gate_up)
    grad_ln_two = jnp.einsum('tcn,dcn->td', grad_gate_up, full_in.astype(jnp.float32))
    gain_two_sum = lax.optimization_barrier(jnp.sum(grad_ln_two * normed_two, axis=0))
    grad_residual = cot_block.astype(jnp.float32) + norm_back(grad_ln_two, gain_two, normed_two, factor_two)
    grad_res_b = grad_residual.astype(jnp.bfloat16)
    grad_ao = fdot(flat_mixed.T, grad_res_b)
    grad_mixed = fdot(grad_res_b, full_ao.T).astype(jnp.bfloat16).reshape(head_shape)
    grad_queries, grad_keys, grad_values = attend_back(queries, key_rows, values, same_doc, log_total, grad_mixed)
    grad_projected = jnp.stack([unrotate(grad_queries, cosine, sine).reshape(group, -1), unrotate(grad_keys, cosine, sine).reshape(group, -1), grad_values.reshape(group, -1)], axis=1).astype(jnp.bfloat16).astype(jnp.float32)
    grad_qkv = jnp.einsum('td,tcn->dcn', ln_one.astype(jnp.float32), grad_projected)
    grad_ln_one = jnp.einsum('tcn,dcn->td', grad_projected, full_qkv.astype(jnp.float32))
    gain_one_sum = lax.optimization_barrier(jnp.sum(grad_ln_one * normed_one, axis=0))
    grad_input = grad_residual + norm_back(grad_ln_one, gain_one, normed_one, factor_one)
    return (output, grad_input, (gain_one_sum, grad_qkv, grad_ao, gain_two_sum, grad_in, grad_mo))

def reference(tokens, seq_lens, g_attn, w_qkv, w_ao, g_mlp, w_in, w_mo, cotangent):
    weights = (g_attn.astype(jnp.float32), w_qkv, w_ao, g_mlp.astype(jnp.float32), w_in, w_mo)
    blocks = tokens.reshape(N_DP, CAP, D)
    cot_blocks = cotangent.reshape(N_DP, CAP, D)
    start = (jnp.zeros((D,), jnp.float32), jnp.zeros((D, 3, D), jnp.float32), jnp.zeros((D, D), jnp.float32), jnp.zeros((D,), jnp.float32), jnp.zeros((D, 2, FF), jnp.float32), jnp.zeros((FF, D), jnp.float32))

    def step_fn(carry, inputs):
        block, cot_block, lengths = inputs
        output, grad_input, grads = group_pass(weights, block, cot_block, lengths)
        carry = tuple((total + part_grad for total, part_grad in zip(carry, grads)))
        return (carry, (output, grad_input))
    totals, (outputs, grad_inputs) = lax.scan(step_fn, start, (blocks, cot_blocks, seq_lens))
    return (outputs.reshape(TOKENS, D), grad_inputs.reshape(TOKENS, D), totals[0], totals[1], totals[2], totals[3], totals[4], totals[5])
```

```python
import math

import jax
import jax.numpy as jnp
from jax import lax
from jax.sharding import PartitionSpec as P

HDIM = 64
ROPE_BASE = 160000.0
BF = jnp.bfloat16
F32 = jnp.float32


def layout(lengths, index):
    ends = jnp.cumsum(lengths)
    passed = ends[None, :] <= index[:, None]
    doc_ids = jnp.sum(passed.astype(jnp.int32), axis=1)
    begins = jnp.max(jnp.where(passed, ends[None, :], jnp.zeros_like(ends)[None, :]), axis=1)
    return (doc_ids, index - begins)


def tables(positions):
    half = HDIM // 2
    rates = jnp.exp(jnp.arange(half, dtype=F32) * (-2.0 * math.log(ROPE_BASE) / HDIM))
    angles = positions.astype(F32)[:, None] * rates[None, :]
    return (jnp.cos(angles)[:, None, :], jnp.sin(angles)[:, None, :])


def rotate(values, cosine, sine):
    half = values.shape[-1] // 2
    first = values[..., :half]
    second = values[..., half:]
    return jnp.concatenate(
        [first * cosine - second * sine, second * cosine + first * sine], axis=-1
    )


def unrotate(grads, cosine, sine):
    return rotate(grads, cosine, -sine)


def normalize(values):
    center = values - jnp.mean(values, axis=-1, keepdims=True)
    factor = lax.rsqrt(jnp.mean(center * center, axis=-1, keepdims=True) + 1e-05)
    return (center * factor, factor)


def norm_back(grad_hat, normed, factor):
    return factor * (
        grad_hat
        - jnp.mean(grad_hat, axis=-1, keepdims=True)
        - normed * jnp.mean(grad_hat * normed, axis=-1, keepdims=True)
    )


def gelu_exact(values):
    return jax.nn.gelu(values, approximate=False)


def ein(spec, left, right):
    return jnp.einsum(spec, left, right, preferred_element_type=F32)


def scores_of(queries, key_rows, same_doc):
    raw = ein("qhd,khd->hqk", queries, key_rows) * 0.125
    return jnp.where(same_doc[None], raw, -1e30)


def attend(queries, key_rows, values, same_doc):
    scores = scores_of(queries, key_rows, same_doc)
    peak = jnp.max(scores, axis=-1, keepdims=True)
    log_total = peak + jnp.log(jnp.sum(jnp.exp(scores - peak), axis=-1, keepdims=True))
    weights = jnp.exp(scores - log_total).astype(BF)
    mixed = ein("hqk,khd->qhd", weights, values)
    return (mixed.astype(BF), log_total)


def attend_back(queries, key_rows, values, same_doc, log_total, grad_out):
    probs = jnp.exp(scores_of(queries, key_rows, same_doc) - log_total)
    grad_values = ein("hqk,qhd->khd", probs.astype(BF), grad_out)
    grad_probs = ein("qhd,khd->hqk", grad_out, values)
    inner = jnp.sum(probs * grad_probs, axis=-1, keepdims=True)
    grad_scores = (probs * (grad_probs - inner) * 0.125).astype(BF)
    grad_queries = ein("hqk,khd->qhd", grad_scores, key_rows)
    grad_keys = ein("hqk,qhd->khd", grad_scores, queries)
    return (grad_queries, grad_keys, grad_values)


class Ring:
    def __init__(self, size):
        self.size = size
        self.chips = size // 2
        self.ringed = self.chips % 2 == 0 and 4 <= self.chips <= 16
        half = self.chips // 2
        order = [2 * p for p in range(half)] + [2 * (self.chips - 1 - p) + 1 for p in range(half, self.chips)]
        self.forward = self.pairs(order, 1)
        self.backward = self.pairs(order, -1)
        self.core = [(i, i ^ 1) for i in range(size)]
        self.groups = [[i for i in range(size) if i % 2 == c] for c in range(2)]

    def pairs(self, order, step):
        n = self.chips
        return [
            (2 * order[k] + c, 2 * order[(k + step) % n] + c) for k in range(n) for c in range(2)
        ]

    def arrival(self, rows):
        me = lax.axis_index("dp")
        chip, core = me // 2, me % 2
        n, half = self.chips, self.chips // 2
        place = jnp.arange(self.size * rows, dtype=jnp.int32)
        other = place // (n * rows)
        block = (place // rows) % n
        if self.ringed:
            spot = jnp.where(chip % 2 == 0, chip // 2, n - 1 - chip // 2)
            offset = jnp.where(block % 2 == 1, -((block + 1) // 2), block // 2)
            where_at = (spot + offset + n) % n
            source = jnp.where(where_at < half, 2 * where_at, 2 * (n - 1 - where_at) + 1)
        else:
            source = block
        return (source * 2 + (core + other) % 2) * rows + place % rows

    def gather(self, block):
        if self.ringed:
            rows = block.shape[1]
            ahead = back = block
            pieces = [block]
            for _ in range(self.chips // 2 - 1):
                ahead = lax.ppermute(ahead, "dp", self.forward)
                back = lax.ppermute(back, "dp", self.backward)
                pieces += [ahead, back]
            pieces.append(lax.ppermute(ahead[:, : rows // 2], "dp", self.forward))
            pieces.append(lax.ppermute(back[:, rows // 2 :], "dp", self.backward))
            own = jnp.concatenate(pieces, axis=1)
        else:
            own = lax.all_gather(
                block, "dp", axis=1, tiled=True, axis_index_groups=self.groups
            )
        return own, lax.ppermute(own, "dp", self.core)

    def reduce(self, own, other):
        theirs = lax.ppermute(other, "dp", self.core)
        n = self.chips
        rows = own.shape[1] // n
        if not self.ringed:
            total = own.astype(F32) + theirs.astype(F32)
            return lax.psum_scatter(
                total, "dp", scatter_dimension=1, tiled=True, axis_index_groups=self.groups
            )

        def mine(j, lo, hi):
            at = slice(j * rows + lo, j * rows + hi)
            return own[:, at].astype(F32) + theirs[:, at].astype(F32)

        h = rows // 2
        down = lax.ppermute(mine(n - 1, 0, h).astype(BF), "dp", self.backward)
        up = lax.ppermute(mine(n - 1, h, rows).astype(BF), "dp", self.forward)
        for step in range(n // 2 - 1, 0, -1):
            a, b = mine(2 * step - 1, 0, rows), mine(2 * step, 0, rows)
            if step == n // 2 - 1:
                a = jnp.concatenate([a[:, :h] + down.astype(F32), a[:, h:]], axis=1)
                b = jnp.concatenate([b[:, :h], b[:, h:] + up.astype(F32)], axis=1)
            else:
                a, b = a + down.astype(F32), b + up.astype(F32)
            down = lax.ppermute(a.astype(BF), "dp", self.backward)
            up = lax.ppermute(b.astype(BF), "dp", self.forward)
        return mine(0, 0, rows) + down.astype(F32) + up.astype(F32)


SWAP = [(0, 1), (1, 0)]


def swap(block):
    return lax.ppermute(block, "tensor", SWAP)


def both_rows(block):
    return jnp.concatenate([block, swap(block)], axis=0)


def sum_rows(full):
    count = full.shape[0] // 2
    return full[:count] + swap(full[count:].astype(BF)).astype(F32)


def body(tokens, seq_lens, g_attn, w_qkv, w_ao, g_mlp, w_in, w_mo, cotangent):
    ring = Ring(lax.axis_size("dp"))
    rows = w_qkv.shape[0]
    count = tokens.shape[0]
    side = lax.axis_index("tensor")
    group = 2 * count
    width = tokens.shape[1]
    cut = width // 2

    gain_one = g_attn.astype(F32)
    gain_two = g_mlp.astype(F32)
    plain_qkv = jnp.transpose(w_qkv, (1, 0, 2)).astype(F32)
    plain_in = jnp.transpose(w_in, (1, 0, 2)).astype(F32)
    block_a = jnp.concatenate(
        [(plain_qkv * gain_one[None, :, None]).astype(BF), w_ao.T[None]], axis=0
    )
    block_b = jnp.concatenate(
        [(plain_in * gain_two[None, :, None]).astype(BF), w_mo.T[None]], axis=0
    )
    own_a, oth_a = ring.gather(block_a)
    own_b, oth_b = ring.gather(block_b)

    index = (jnp.arange(group, dtype=jnp.int32) + side * count) % group
    doc_ids, positions = layout(seq_lens[0], index)
    same_doc = doc_ids[:, None] == doc_ids[None, :]
    cosine, sine = tables(positions)

    places = ring.arrival(rows)
    chosen = (jnp.arange(width, dtype=jnp.int32)[:, None] == places[None, :]).astype(BF)
    moved = ein("td,de->te", jnp.concatenate([tokens, cotangent], axis=0), chosen).astype(BF)
    moved_other = swap(moved)
    tokens_all = jnp.concatenate([moved[:count], moved_other[:count]], axis=0).astype(F32)
    cot_all = jnp.concatenate([moved[count:], moved_other[count:]], axis=0)

    def into(acts, own, oth, spec):
        return ein(spec, acts[:, :cut], own) + ein(spec, acts[:, cut:], oth)

    def outof(acts, own, oth, spec):
        return jnp.concatenate([ein(spec, acts, own), ein(spec, acts, oth)], axis=1)

    local_heads = w_qkv.shape[2] // HDIM
    head_shape = (group, local_heads, HDIM)
    normed_all, factor_all = normalize(tokens_all)
    normed_one, factor_one = normed_all[:count], factor_all[:count]
    hat_one = normed_all.astype(BF)
    projected = into(hat_one, own_a[:3], oth_a[:3], "td,cdn->ctn")
    queries = rotate(projected[0].reshape(head_shape), cosine, sine).astype(BF)
    key_rows = rotate(projected[1].reshape(head_shape), cosine, sine).astype(BF)
    values = projected[2].reshape(head_shape).astype(BF)
    mixed, log_total = attend(queries, key_rows, values, same_doc)
    flat_mixed = mixed.reshape(group, -1)
    residual = tokens_all[:count] + sum_rows(outof(flat_mixed, own_a[3], oth_a[3], "tn,dn->td"))
    normed_two, factor_two = normalize(residual)
    hat_two = both_rows(normed_two.astype(BF))
    gate = into(hat_two, own_b[0], oth_b[0], "td,df->tf")
    upper = into(hat_two, own_b[1], oth_b[1], "td,df->tf")
    product = (gelu_exact(gate) * upper).astype(BF)
    output = (residual + sum_rows(outof(product, own_b[2], oth_b[2], "tf,df->td"))).astype(BF)
    output = ein("te,de->td", output, chosen).astype(BF)

    grad_product = into(cot_all, own_b[2], oth_b[2], "td,df->tf")
    activated, pull = jax.vjp(gelu_exact, gate)
    grad_gate = pull(grad_product * upper)[0].astype(BF)
    grad_upper = (grad_product * activated).astype(BF)

    def weight_grads(acts, grads):
        return [ein("td,tf->df", acts, g).astype(BF) for g in grads]

    def pair(items):
        left, right = [], []
        for acts, grads in items:
            left += weight_grads(acts[:, :cut], grads)
            right += weight_grads(acts[:, cut:], grads)
        return jnp.stack(left), jnp.stack(right)

    raw_b = ring.reduce(*pair([(hat_two, [grad_gate, grad_upper]), (cot_all, [product])]))
    grad_hat_two = sum_rows(
        outof(grad_gate, own_b[0], oth_b[0], "tf,df->td")
        + outof(grad_upper, own_b[1], oth_b[1], "tf,df->td")
    )
    grad_residual = moved[count:].astype(F32) + norm_back(grad_hat_two, normed_two, factor_two)
    grad_res_all = both_rows(grad_residual.astype(BF))
    grad_mixed = (
        into(grad_res_all, own_a[3], oth_a[3], "td,dn->tn").astype(BF).reshape(head_shape)
    )
    grad_queries, grad_keys, grad_values = attend_back(
        queries, key_rows, values, same_doc, log_total, grad_mixed
    )
    grad_proj = [
        unrotate(grad_queries, cosine, sine).reshape(group, -1).astype(BF),
        unrotate(grad_keys, cosine, sine).reshape(group, -1).astype(BF),
        grad_values.reshape(group, -1).astype(BF),
    ]
    raw_a = ring.reduce(*pair([(hat_one, grad_proj), (grad_res_all, [flat_mixed])]))
    stacked = jnp.stack(grad_proj)
    grad_hat_one = sum_rows(outof(stacked, own_a[:3], oth_a[:3], "ctn,cdn->td"))
    grad_input = grad_residual + norm_back(grad_hat_one, normed_one, factor_one)
    top = lax.reduce_precision(grad_input, 8, 7)
    middle = lax.reduce_precision(grad_input - top, 8, 7)
    parts = jnp.concatenate([top, middle, grad_input - top - middle], axis=0).astype(BF)
    spread = ein("te,de->td", parts, chosen)
    grad_input = spread[:count] + spread[count : 2 * count] + spread[2 * count :]

    gain_sums = jnp.stack(
        [jnp.sum(plain_qkv * raw_a[:3], axis=(0, 2)), jnp.sum(plain_in * raw_b[:2], axis=(0, 2))]
    )
    part = rows // 2
    gain_shares = lax.dynamic_slice_in_dim(gain_sums, side * part, part, 1) + swap(
        lax.dynamic_slice_in_dim(gain_sums, (1 - side) * part, part, 1)
    )
    return (
        output,
        grad_input,
        gain_shares[0],
        jnp.transpose(raw_a[:3] * gain_one[None, :, None], (1, 0, 2)),
        raw_a[3].T,
        gain_shares[1],
        jnp.transpose(raw_b[:2] * gain_two[None, :, None], (1, 0, 2)),
        raw_b[2].T,
    )


def solution(mesh):
    return jax.shard_map(
        body,
        mesh=mesh,
        in_specs=(
            P(("dp", "tensor"), None),
            P("dp", None),
            P("dp"),
            P("dp", None, "tensor"),
            P("tensor", "dp"),
            P("dp"),
            P("dp", None, "tensor"),
            P("tensor", "dp"),
            P(("dp", "tensor"), None),
        ),
        out_specs=(
            P(("dp", "tensor"), None),
            P(("dp", "tensor"), None),
            P(("dp", "tensor")),
            P("dp", None, "tensor"),
            P("tensor", "dp"),
            P(("dp", "tensor")),
            P("dp", None, "tensor"),
            P("tensor", "dp"),
        ),
        check_vma=False,
    )
```

```python
import math

import jax
import jax.numpy as jnp
from jax import lax
from jax.experimental import pallas as pl
from jax.experimental.pallas import tpu as pltpu
from jax.sharding import PartitionSpec as P

HDIM = 64
ROPE_BASE = 160000.0
BF = jnp.bfloat16
F32 = jnp.float32


def layout(lengths, index):
    ends = jnp.cumsum(lengths)
    passed = ends[None, :] <= index[:, None]
    doc_ids = jnp.sum(passed.astype(jnp.int32), axis=1)
    begins = jnp.max(jnp.where(passed, ends[None, :], jnp.zeros_like(ends)[None, :]), axis=1)
    return (doc_ids, index - begins)


def tables(positions, lanes):
    half = HDIM // 2
    lane = jnp.arange(lanes, dtype=jnp.int32)
    rates = jnp.exp((lane % half).astype(F32) * (-2.0 * math.log(ROPE_BASE) / HDIM))
    angles = positions.astype(F32)[:, None] * rates[None, :]
    sign = jnp.where(lane % HDIM < half, -1.0, 1.0)
    return jnp.cos(angles), jnp.sin(angles) * sign[None, :]


def normalize(values):
    center = values - jnp.mean(values, axis=-1, keepdims=True)
    factor = lax.rsqrt(jnp.mean(center * center, axis=-1, keepdims=True) + 1e-05)
    return (center * factor, factor)


def norm_back(grad_hat, normed, factor):
    return factor * (
        grad_hat
        - jnp.mean(grad_hat, axis=-1, keepdims=True)
        - normed * jnp.mean(grad_hat * normed, axis=-1, keepdims=True)
    )


def ein(spec, left, right):
    return jnp.einsum(spec, left, right, preferred_element_type=F32)


def nn(left, right):
    return jnp.dot(left, right, preferred_element_type=F32)


def nt(left, right):
    return lax.dot_general(left, right, (((1,), (1,)), ((), ())), preferred_element_type=F32)


def tn(left, right):
    return lax.dot_general(left, right, (((0,), (0,)), ((), ())), preferred_element_type=F32)


def shape(dims, kind):
    return jax.ShapeDtypeStruct(dims, kind)


ANYWHERE = pl.BlockSpec(memory_space=pl.ANY)
WHOLE = pl.BlockSpec(memory_space=pltpu.VMEM)


def load_planes(own_hbm, oth_hbm, own, oth, sems):
    copies = []
    for plane in range(own.shape[0]):
        pair = (
            pltpu.make_async_copy(own_hbm.at[plane], own.at[plane], sems.at[0, plane]),
            pltpu.make_async_copy(oth_hbm.at[plane], oth.at[plane], sems.at[1, plane]),
        )
        copies.append(pair)
    return copies


def begin(copies, order):
    for plane in order:
        copies[plane][0].start()
        copies[plane][1].start()


def finish(copies, plane):
    copies[plane][0].wait()
    copies[plane][1].wait()


def planes_scratch(block):
    return [
        pltpu.VMEM(block, BF),
        pltpu.VMEM(block, BF),
        pltpu.SemaphoreType.DMA((2, block[0])),
    ]


def swing(values, cosine, sine):
    lanes = values.shape[-1]
    half = HDIM // 2
    lane = lax.broadcasted_iota(jnp.int32, values.shape, 1)
    turned = jnp.where(
        lane % HDIM < half,
        pltpu.roll(values, lanes - half, 1),
        pltpu.roll(values, half, 1),
    )
    return values * cosine + turned * sine


def head_probs(query, key, same):
    scores = jnp.where(same, nt(query, key) * 0.125, -1e30)
    peak = jnp.max(scores, axis=-1, keepdims=True)
    raised = jnp.exp(scores - peak)
    return raised * (1.0 / jnp.sum(raised, axis=-1, keepdims=True))


def attend_kernel(x, own_hbm, oth_hbm, docs, docs_row, cos, sin, qkv, mixed, hat, part, away, own, oth, sems):
    copies = load_planes(own_hbm, oth_hbm, own, oth, sems)
    begin(copies, range(4))
    normed, _ = normalize(x[...].astype(F32))
    hat[...] = normed.astype(BF)
    cut = own.shape[1]
    count = part.shape[0]
    for plane in range(3):
        finish(copies, plane)
        value = nn(hat[:, :cut], own[plane]) + nn(hat[:, cut:], oth[plane])
        if plane < 2:
            value = swing(value, cos[...], sin[...])
        qkv[plane] = value.astype(BF)
    same = docs[...] == docs_row[...]
    for head in range(qkv.shape[2] // HDIM):
        at = slice(head * HDIM, (head + 1) * HDIM)
        probs = head_probs(qkv[0, :, at], qkv[1, :, at], same)
        mixed[:, at] = nn(probs.astype(BF), qkv[2, :, at]).astype(BF)
    finish(copies, 3)
    for weights, lo in ((own, 0), (oth, cut)):
        full = nt(mixed[...], weights[3])
        part[:, lo : lo + cut] = full[:count]
        away[:, lo : lo + cut] = full[count:].astype(BF)


def attend_call(x, own, oth, docs, cos, sin):
    group, width = x.shape
    planes, cut, lanes = own.shape
    return pl.pallas_call(
        attend_kernel,
        out_shape=(
            shape((3, group, lanes), BF),
            shape((group, lanes), BF),
            shape((group, width), BF),
            shape((group // 2, width), F32),
            shape((group // 2, width), BF),
        ),
        in_specs=[WHOLE, ANYWHERE, ANYWHERE, WHOLE, WHOLE, WHOLE, WHOLE],
        out_specs=(WHOLE,) * 5,
        scratch_shapes=planes_scratch(own.shape),
        name="attend",
    )(x, own, oth, docs[:, None], docs[None, :], cos, sin)


def mlp_kernel(hat, cot, own_hbm, oth_hbm, three, part, away, out_part, out_away, own, oth, sems, gate, upper, back):
    copies = load_planes(own_hbm, oth_hbm, own, oth, sems)
    begin(copies, range(3))
    cut = own.shape[1]
    count = part.shape[0]
    finish(copies, 0)
    gate[...] = nn(hat[:, :cut], own[0]) + nn(hat[:, cut:], oth[0])
    finish(copies, 1)
    upper[...] = nn(hat[:, :cut], own[1]) + nn(hat[:, cut:], oth[1])
    finish(copies, 2)
    back[...] = nn(cot[:, :cut], own[2]) + nn(cot[:, cut:], oth[2])
    step = 16

    def chunk(i, carry):
        at = pl.ds(pl.multiple_of(i * step, step), step)
        v, u, g = gate[at, :], upper[at, :], back[at, :]
        share = 0.5 * (1.0 + lax.erf(v * (1.0 / math.sqrt(2.0))))
        slope = share + v * (jnp.exp(-0.5 * v * v) * (1.0 / math.sqrt(2.0 * math.pi)))
        active = v * share
        three[0, at, :] = (g * u * slope).astype(BF)
        three[1, at, :] = (g * active).astype(BF)
        three[2, at, :] = (active * u).astype(BF)
        return carry

    lax.fori_loop(0, gate.shape[0] // step, chunk, 0)
    for weights, lo in ((own, 0), (oth, cut)):
        full = nt(three[0], weights[0]) + nt(three[1], weights[1])
        part[:, lo : lo + cut] = full[:count]
        away[:, lo : lo + cut] = full[count:].astype(BF)
        full = nt(three[2], weights[2])
        out_part[:, lo : lo + cut] = full[:count]
        out_away[:, lo : lo + cut] = full[count:].astype(BF)


def mlp_call(hat, cot, own, oth):
    group, width = hat.shape
    hidden = own.shape[2]
    half = group // 2
    return pl.pallas_call(
        mlp_kernel,
        out_shape=(
            shape((3, group, hidden), BF),
            shape((half, width), F32),
            shape((half, width), BF),
            shape((half, width), F32),
            shape((half, width), BF),
        ),
        in_specs=[WHOLE, WHOLE, ANYWHERE, ANYWHERE],
        out_specs=(WHOLE,) * 5,
        scratch_shapes=planes_scratch(own.shape) + [pltpu.VMEM((group, hidden), F32)] * 3,
        name="mlp",
    )(hat, cot, own, oth)


def back_kernel(grad, qkv, own_hbm, oth_hbm, docs, docs_row, cos, sin, three, part, away, own, oth, sems, gmix, wide):
    copies = load_planes(own_hbm, oth_hbm, own, oth, sems)
    begin(copies, (3, 0, 1, 2))
    cut = own.shape[1]
    count = part.shape[0]
    finish(copies, 3)
    gmix[...] = (nn(grad[:, :cut], own[3]) + nn(grad[:, cut:], oth[3])).astype(BF)
    same = docs[...] == docs_row[...]
    for head in range(qkv.shape[2] // HDIM):
        at = slice(head * HDIM, (head + 1) * HDIM)
        query, key, value, outer = qkv[0, :, at], qkv[1, :, at], qkv[2, :, at], gmix[:, at]
        probs = head_probs(query, key, same)
        three[2, :, at] = tn(probs.astype(BF), outer).astype(BF)
        grad_probs = nt(outer, value)
        inner = jnp.sum(probs * grad_probs, axis=-1, keepdims=True)
        grad_scores = (probs * (grad_probs - inner) * 0.125).astype(BF)
        wide[0, :, at] = nn(grad_scores, key)
        wide[1, :, at] = tn(grad_scores, query)
    for plane in range(2):
        three[plane] = swing(wide[plane], cos[...], -sin[...]).astype(BF)
    for plane in range(3):
        finish(copies, plane)
    for weights, lo in ((own, 0), (oth, cut)):
        full = nt(three[0], weights[0]) + nt(three[1], weights[1]) + nt(three[2], weights[2])
        part[:, lo : lo + cut] = full[:count]
        away[:, lo : lo + cut] = full[count:].astype(BF)


def back_call(grad, qkv, own, oth, docs, cos, sin):
    group, width = grad.shape
    lanes = own.shape[2]
    return pl.pallas_call(
        back_kernel,
        out_shape=(
            shape((3, group, lanes), BF),
            shape((group // 2, width), F32),
            shape((group // 2, width), BF),
        ),
        in_specs=[WHOLE, WHOLE, ANYWHERE, ANYWHERE, WHOLE, WHOLE, WHOLE, WHOLE],
        out_specs=(WHOLE,) * 3,
        scratch_shapes=planes_scratch(own.shape)
        + [pltpu.VMEM((group, lanes), BF), pltpu.VMEM((2, group, lanes), F32)],
        name="attend_back",
    )(grad, qkv, own, oth, docs[:, None], docs[None, :], cos, sin)


def outer_kernel(first, second, three, last, out):
    plane = pl.program_id(0)
    split = pl.num_programs(0) - 1

    @pl.when(plane < split)
    def _():
        out[0] = tn(first[...], three[0]).astype(BF)

    @pl.when(plane == split)
    def _():
        out[0] = tn(second[...], last[...]).astype(BF)


def weight_grads(first, second, three, last, side):
    group, width = first.shape
    cut = width // 2
    lanes = three.shape[2]
    merged = last is None
    planes = 3 if merged else 4
    last_spec = pl.BlockSpec((group, lanes), lambda i: (0, 0))
    if merged:
        last = three
        last_spec = pl.BlockSpec((None, group, lanes), lambda i: (2, 0, 0))
    return pl.pallas_call(
        outer_kernel,
        grid=(planes,),
        out_shape=shape((planes, cut, lanes), BF),
        in_specs=[
            pl.BlockSpec((group, cut), lambda i: (0, side)),
            pl.BlockSpec((group, cut), lambda i: (0, side)),
            pl.BlockSpec((1, group, lanes), lambda i: (jnp.minimum(i, planes - 2), 0, 0)),
            last_spec,
        ],
        out_specs=pl.BlockSpec((1, cut, lanes), lambda i: (i, 0, 0)),
        name="weight_grads",
    )(first, second, three, last)


def first_kernel(own, theirs, down, up):
    total = (own[...].astype(F32) + theirs[...].astype(F32)).astype(BF)
    h = total.shape[1] // 2
    down[...] = total[:, :h]
    up[...] = total[:, h:]


def first_call(own, theirs, rows, j):
    planes, _, lanes = own.shape
    block = pl.BlockSpec((1, rows, lanes), lambda i: (i, j, 0))
    out = pl.BlockSpec((1, rows // 2, lanes), lambda i: (i, 0, 0))
    return pl.pallas_call(
        first_kernel,
        grid=(planes,),
        out_shape=(shape((planes, rows // 2, lanes), BF),) * 2,
        in_specs=[block, block],
        out_specs=(out, out),
        name="ring_first",
    )(own, theirs)


def middle_kernel(own_a, theirs_a, own_b, theirs_b, down, up, out_a, out_b):
    a = own_a[...].astype(F32) + theirs_a[...].astype(F32)
    b = own_b[...].astype(F32) + theirs_b[...].astype(F32)
    rows = a.shape[1]
    h = down.shape[1]
    if h == rows:
        out_a[...] = (a + down[...].astype(F32)).astype(BF)
        out_b[...] = (b + up[...].astype(F32)).astype(BF)
    else:
        out_a[:, :h] = (a[:, :h] + down[...].astype(F32)).astype(BF)
        out_a[:, h:] = a[:, h:].astype(BF)
        out_b[:, :h] = b[:, :h].astype(BF)
        out_b[:, h:] = (b[:, h:] + up[...].astype(F32)).astype(BF)


def middle_call(own, theirs, down, up, rows, j):
    planes, _, lanes = own.shape
    left = pl.BlockSpec((1, rows, lanes), lambda i: (i, j, 0))
    right = pl.BlockSpec((1, rows, lanes), lambda i: (i, j + 1, 0))
    got = pl.BlockSpec((1, down.shape[1], lanes), lambda i: (i, 0, 0))
    out = pl.BlockSpec((1, rows, lanes), lambda i: (i, 0, 0))
    return pl.pallas_call(
        middle_kernel,
        grid=(planes,),
        out_shape=(shape((planes, rows, lanes), BF),) * 2,
        in_specs=[left, left, right, right, got, got],
        out_specs=(out, out),
        name="ring_middle",
    )(own, theirs, own, theirs, down, up)


def last_kernel(own, theirs, down, up, out):
    out[...] = (own[...].astype(F32) + theirs[...].astype(F32)) + (
        down[...].astype(F32) + up[...].astype(F32)
    )


def last_call(own, theirs, down, up, rows):
    planes, _, lanes = own.shape
    block = pl.BlockSpec((1, rows, lanes), lambda i: (i, 0, 0))
    return pl.pallas_call(
        last_kernel,
        grid=(planes,),
        out_shape=shape((planes, rows, lanes), F32),
        in_specs=[block] * 4,
        out_specs=block,
        name="ring_last",
    )(own, theirs, down, up)


def tie(value, *after):
    return lax.optimization_barrier((value, after))[0]


class Ring:
    def __init__(self, size):
        self.size = size
        self.chips = size // 2
        self.ringed = self.chips % 2 == 0 and 4 <= self.chips <= 16
        half = self.chips // 2
        order = [2 * p for p in range(half)] + [2 * (self.chips - 1 - p) + 1 for p in range(half, self.chips)]
        self.forward = self.pairs(order, 1)
        self.backward = self.pairs(order, -1)
        self.core = [(i, i ^ 1) for i in range(size)]
        self.groups = [[i for i in range(size) if i % 2 == c] for c in range(2)]

    def pairs(self, order, step):
        n = self.chips
        return [
            (2 * order[k] + c, 2 * order[(k + step) % n] + c) for k in range(n) for c in range(2)
        ]

    def arrival(self, rows):
        me = lax.axis_index("dp")
        chip, core = me // 2, me % 2
        n, half = self.chips, self.chips // 2
        place = jnp.arange(self.size * rows, dtype=jnp.int32)
        other = place // (n * rows)
        block = (place // rows) % n
        if self.ringed:
            spot = jnp.where(chip % 2 == 0, chip // 2, n - 1 - chip // 2)
            offset = jnp.where(block % 2 == 1, -((block + 1) // 2), block // 2)
            where_at = (spot + offset + n) % n
            source = jnp.where(where_at < half, 2 * where_at, 2 * (n - 1 - where_at) + 1)
        else:
            source = block
        return (source * 2 + (core + other) % 2) * rows + place % rows

    def ahead(self, block):
        return lax.ppermute(block, "dp", self.forward)

    def back(self, block):
        return lax.ppermute(block, "dp", self.backward)

    def across(self, block):
        return lax.ppermute(block, "dp", self.core)


class Gather:
    def __init__(self, ring, block):
        self.ring = ring
        self.block = block
        self.pieces = [block]
        self.a = self.b = block
        self.left = ring.chips // 2 if ring.ringed else 0

    def step(self, *after):
        if self.left == 0:
            return
        a, b = (tie((self.a, self.b), *after) if after else (self.a, self.b))
        self.left -= 1
        if self.left == 0:
            rows = a.shape[1]
            a, b = a[:, : rows // 2], b[:, rows // 2 :]
        self.a, self.b = self.ring.ahead(a), self.ring.back(b)
        self.pieces += [self.a, self.b]

    def done(self):
        if self.ring.ringed:
            own = jnp.concatenate(self.pieces, axis=1)
        else:
            own = lax.all_gather(
                self.block, "dp", axis=1, tiled=True, axis_index_groups=self.ring.groups
            )
        return own, self.ring.across(own)


class Reduce:
    def __init__(self, ring, own, theirs):
        self.ring, self.own, self.theirs = ring, own, theirs
        self.rows = own.shape[1] // ring.chips
        self.left = ring.chips // 2 if ring.ringed else 0
        self.down = self.up = None
        self.sent = ()

    def step(self, *after):
        if self.left == 0:
            return
        j = 2 * self.left - 1
        if self.down is None:
            down, up = first_call(self.own, self.theirs, self.rows, j)
        else:
            down, up = middle_call(self.own, self.theirs, self.down, self.up, self.rows, j)
        if after:
            down, up = tie((down, up), *after)
        self.left -= 1
        self.sent = (down, up)
        self.down, self.up = self.ring.back(down), self.ring.ahead(up)

    def done(self, *after):
        if not self.ring.ringed:
            total = self.own.astype(F32) + self.theirs.astype(F32)
            return lax.psum_scatter(
                total, "dp", scatter_dimension=1, tiled=True, axis_index_groups=self.ring.groups
            )
        own = tie(self.own, *after) if after else self.own
        return last_call(own, self.theirs, self.down, self.up, self.rows)


def swap(block):
    return lax.ppermute(block, "tensor", [(0, 1), (1, 0)])


def body(tokens, seq_lens, g_attn, w_qkv, w_ao, g_mlp, w_in, w_mo, cotangent):
    ring = Ring(lax.axis_size("dp"))
    rows = w_qkv.shape[0]
    count = tokens.shape[0]
    side = lax.axis_index("tensor")
    group = 2 * count
    width = tokens.shape[1]

    gain_one = g_attn.astype(F32)
    gain_two = g_mlp.astype(F32)
    plain_qkv = jnp.transpose(w_qkv, (1, 0, 2)).astype(F32)
    plain_in = jnp.transpose(w_in, (1, 0, 2)).astype(F32)
    block_a = jnp.concatenate(
        [(plain_qkv * gain_one[None, :, None]).astype(BF), w_ao.T[None]], axis=0
    )
    hidden = w_in.shape[2]
    block_b = jnp.concatenate(
        [(plain_in * gain_two[None, :, None]).astype(BF), w_mo.T[None]], axis=0
    )
    block_b = jnp.pad(block_b, ((0, 0), (0, 0), (0, -hidden % 128)))
    gather_a = Gather(ring, block_a)
    gather_a.step()
    gather_b = Gather(ring, tie(block_b, block_a))
    gather_b.step()

    index = (jnp.arange(group, dtype=jnp.int32) + side * count) % group
    docs, positions = layout(seq_lens[0], index)
    cosine, sine = tables(positions, w_qkv.shape[2])

    places = ring.arrival(rows)
    chosen = (jnp.arange(width, dtype=jnp.int32)[:, None] == places[None, :]).astype(BF)
    moved = ein("td,de->te", jnp.concatenate([tokens, cotangent], axis=0), chosen).astype(BF)
    moved_other = swap(moved)
    tokens_all = jnp.concatenate([moved[:count], moved_other[:count]], axis=0)
    cot_all = jnp.concatenate([moved[count:], moved_other[count:]], axis=0)

    gather_a.step(moved)
    gather_a.step(cosine, sine)
    gather_b.step(*gather_a.pieces[3:5])
    gather_a.step(tokens_all, cot_all)
    own_a, oth_a = gather_a.done()

    normed_one, factor_one = normalize(moved[:count].astype(F32))
    qkv, mixed, hat_one, part, away = attend_call(tokens_all, own_a, oth_a, docs, cosine, sine)
    swapped = swap(away)
    gather_b.step(away)
    residual = moved[:count].astype(F32) + part + swapped.astype(F32)
    normed_two, factor_two = normalize(residual)
    hat_own = normed_two.astype(BF)
    hat_two = jnp.concatenate([hat_own, swap(hat_own)], axis=0)
    gather_b.step(hat_own)
    own_b, oth_b = gather_b.done()

    three_b, part, away, out_part, out_away = mlp_call(hat_two, cot_all, own_b, oth_b)
    swapped = swap(away)
    side_b = weight_grads(hat_two, cot_all, three_b, None, 1)
    cross_b = ring.across(side_b)
    main_b = weight_grads(tie(hat_two, side_b), cot_all, three_b, None, 0)
    reduce_b = Reduce(ring, main_b, cross_b)
    reduce_b.step()
    grad_hat_two = part + tie(swapped, *reduce_b.sent).astype(F32)
    grad_residual = moved[count:].astype(F32) + norm_back(grad_hat_two, normed_two, factor_two)
    grad_res_own = grad_residual.astype(BF)
    grad_res_all = jnp.concatenate([grad_res_own, swap(grad_res_own)], axis=0)
    reduce_b.step(grad_res_own)
    three_a, part, away = back_call(
        tie(grad_res_all, *reduce_b.sent), qkv, own_a, oth_a, docs, cosine, sine
    )
    reduce_b.step(away)
    swapped = swap(away)
    side_a = weight_grads(tie(hat_one, *reduce_b.sent), grad_res_all, three_a, mixed, 1)
    cross_a = ring.across(side_a)
    main_a = weight_grads(tie(hat_one, side_a), grad_res_all, three_a, mixed, 0)
    reduce_a = Reduce(ring, main_a, cross_a)
    reduce_a.step()
    reduce_b.step(*reduce_a.sent)
    reduce_a.step(*reduce_b.sent)
    raw_b = reduce_b.done(*reduce_a.sent)

    grad_hat_one = part + tie(swapped, *reduce_a.sent).astype(F32)
    grad_input = grad_residual + norm_back(grad_hat_one, normed_one, factor_one)
    top = lax.reduce_precision(grad_input, 8, 7)
    middle = lax.reduce_precision(grad_input - top, 8, 7)
    parts = jnp.concatenate([top, middle, grad_input - top - middle], axis=0).astype(BF)
    spread = ein("te,de->td", parts, chosen)
    grad_input = spread[:count] + spread[count : 2 * count] + spread[2 * count :]
    out_swapped = swap(tie(out_away, swapped))
    reduce_a.step(grad_input)

    raw_b = tie(raw_b, *reduce_a.sent)[:, :, :hidden]
    grad_in = jnp.transpose(raw_b[:2] * gain_two[None, :, None], (1, 0, 2))
    grad_mo = raw_b[2].T
    gain_two_sum = jnp.sum(plain_in * raw_b[:2], axis=(0, 2))
    reduce_a.step(grad_in, grad_mo, gain_two_sum)
    output = (residual + out_part + tie(out_swapped, *reduce_a.sent).astype(F32)).astype(BF)
    output = ein("te,de->td", output, chosen).astype(BF)
    raw_a = reduce_a.done()

    gain_sums = jnp.stack(
        [jnp.sum(plain_qkv * raw_a[:3], axis=(0, 2)), gain_two_sum]
    )
    share = rows // 2
    gain_shares = lax.dynamic_slice_in_dim(gain_sums, side * share, share, 1) + swap(
        lax.dynamic_slice_in_dim(gain_sums, (1 - side) * share, share, 1)
    )
    return (
        output,
        grad_input,
        gain_shares[0],
        jnp.transpose(raw_a[:3] * gain_one[None, :, None], (1, 0, 2)),
        raw_a[3].T,
        gain_shares[1],
        grad_in,
        grad_mo,
    )


def solution(mesh):
    return jax.shard_map(
        body,
        mesh=mesh,
        in_specs=(
            P(("dp", "tensor"), None),
            P("dp", None),
            P("dp"),
            P("dp", None, "tensor"),
            P("tensor", "dp"),
            P("dp"),
            P("dp", None, "tensor"),
            P("tensor", "dp"),
            P(("dp", "tensor"), None),
        ),
        out_specs=(
            P(("dp", "tensor"), None),
            P(("dp", "tensor"), None),
            P(("dp", "tensor")),
            P("dp", None, "tensor"),
            P("tensor", "dp"),
            P(("dp", "tensor")),
            P("dp", None, "tensor"),
            P("tensor", "dp"),
        ),
        check_vma=False,
    )
```

```python
import math

import jax
import jax.numpy as jnp
from jax import lax
from jax.experimental import pallas as pl
from jax.experimental.pallas import tpu as pltpu
from jax.sharding import PartitionSpec as P

HDIM = 64
ROPE_BASE = 160000.0
BF = jnp.bfloat16
F32 = jnp.float32


def layout(lengths, index):
    ends = jnp.cumsum(lengths)
    passed = ends[None, :] <= index[:, None]
    doc_ids = jnp.sum(passed.astype(jnp.int32), axis=1)
    begins = jnp.max(jnp.where(passed, ends[None, :], jnp.zeros_like(ends)[None, :]), axis=1)
    return (doc_ids, index - begins)


def tables(positions, lanes):
    half = HDIM // 2
    lane = jnp.arange(lanes, dtype=jnp.int32)
    rates = jnp.exp((lane % half).astype(F32) * (-2.0 * math.log(ROPE_BASE) / HDIM))
    angles = positions.astype(F32)[:, None] * rates[None, :]
    sign = jnp.where(lane % HDIM < half, -1.0, 1.0)
    return jnp.cos(angles), jnp.sin(angles) * sign[None, :]


def normalize(values):
    center = values - jnp.mean(values, axis=-1, keepdims=True)
    factor = lax.rsqrt(jnp.mean(center * center, axis=-1, keepdims=True) + 1e-05)
    return (center * factor, factor)


def norm_back(grad_hat, normed, factor):
    return factor * (
        grad_hat
        - jnp.mean(grad_hat, axis=-1, keepdims=True)
        - normed * jnp.mean(grad_hat * normed, axis=-1, keepdims=True)
    )


def ein(spec, left, right):
    return jnp.einsum(spec, left, right, preferred_element_type=F32)


def nn(left, right):
    return jnp.dot(left, right, preferred_element_type=F32)


def nt(left, right):
    return lax.dot_general(left, right, (((1,), (1,)), ((), ())), preferred_element_type=F32)


def tn(left, right):
    return lax.dot_general(left, right, (((0,), (0,)), ((), ())), preferred_element_type=F32)


def shape(dims, kind):
    return jax.ShapeDtypeStruct(dims, kind)


ANYWHERE = pl.BlockSpec(memory_space=pltpu.HBM)
LONG = pl.CostEstimate(flops=10**11, bytes_accessed=10**9, transcendentals=0)
NEAR = 2**20
SHORT = pl.CostEstimate(flops=1000, bytes_accessed=1000, transcendentals=0)
WHOLE = pl.BlockSpec(memory_space=pltpu.VMEM)


def load_planes(parts, own, oth, sems):
    half = len(parts) // 2
    copies = []
    for plane in range(own.shape[0]):
        copies.append([])
        for k, part in enumerate(parts):
            at = sum(q.shape[1] for q in parts[k // half * half : k])
            target = (own if k < half else oth).at[plane, pl.ds(at, part.shape[1])]
            copies[plane].append(pltpu.make_async_copy(part.at[plane], target, sems.at[k, plane]))
    return copies


def begin(copies, order):
    for plane in order:
        for copy in copies[plane]:
            copy.start()


def finish(copies, plane):
    for copy in copies[plane]:
        copy.wait()


def held_block(own):
    return (own[0].shape[0], sum(part.shape[1] for part in own), own[0].shape[2])


def planes_scratch(own):
    block = held_block(own)
    return [
        pltpu.VMEM(block, BF),
        pltpu.VMEM(block, BF),
        pltpu.SemaphoreType.DMA((2 * len(own), block[0])),
    ]


def stack_kernel(*refs):
    pieces, out, sems = refs[:-2], refs[-2], refs[-1]
    copies, at = [], 0
    for k, piece in enumerate(pieces):
        copies.append(
            pltpu.make_async_copy(piece, out.at[:, pl.ds(at, piece.shape[1])], sems.at[k])
        )
        copies[k].start()
        at += piece.shape[1]
    for copy in copies:
        copy.wait()


def stack_call(pieces, far):
    planes, _, lanes = pieces[0].shape
    return pl.pallas_call(
        stack_kernel,
        out_shape=shape((planes, sum(p.shape[1] for p in pieces), lanes), BF),
        in_specs=[WHOLE] * len(pieces),
        out_specs=ANYWHERE,
        scratch_shapes=[pltpu.SemaphoreType.DMA((len(pieces),))],
        name="stack_rows",
        cost_estimate=LONG,
    )(*pieces[:far], *[close(piece) for piece in pieces[far:]])


def swing(values, cosine, sine):
    lanes = values.shape[-1]
    half = HDIM // 2
    lane = lax.broadcasted_iota(jnp.int32, values.shape, 1)
    turned = jnp.where(
        lane % HDIM < half,
        pltpu.roll(values, lanes - half, 1),
        pltpu.roll(values, half, 1),
    )
    return values * cosine + turned * sine


def head_probs(query, key, same):
    scores = jnp.where(same, nt(query, key) * 0.125, -1e30)
    peak = jnp.max(scores, axis=-1, keepdims=True)
    raised = jnp.exp(scores - peak)
    return raised * (1.0 / jnp.sum(raised, axis=-1, keepdims=True))


def attend_kernel(x, docs, docs_row, cos, sin, *refs):
    parts, (qkv, mixed, hat, part, away, own, oth, sems) = refs[:-8], refs[-8:]
    copies = load_planes(parts, own, oth, sems)
    begin(copies, range(4))
    normed, _ = normalize(x[...].astype(F32))
    hat[...] = normed.astype(BF)
    cut = own.shape[1]
    count = part.shape[0]
    for plane in range(3):
        finish(copies, plane)
        value = nn(hat[:, :cut], own[plane]) + nn(hat[:, cut:], oth[plane])
        if plane < 2:
            value = swing(value, cos[...], sin[...])
        qkv[plane] = value.astype(BF)
    same = docs[...] == docs_row[...]
    for head in range(qkv.shape[2] // HDIM):
        at = slice(head * HDIM, (head + 1) * HDIM)
        probs = head_probs(qkv[0, :, at], qkv[1, :, at], same)
        mixed[:, at] = nn(probs.astype(BF), qkv[2, :, at]).astype(BF)
    finish(copies, 3)
    for weights, lo in ((own, 0), (oth, cut)):
        full = nt(mixed[...], weights[3])
        part[:, lo : lo + cut] = full[:count]
        away[:, lo : lo + cut] = full[count:].astype(BF)


def attend_call(x, own, oth, docs, cos, sin):
    group, width = x.shape
    lanes = own[0].shape[2]
    return pl.pallas_call(
        attend_kernel,
        out_shape=(
            shape((3, group, lanes), BF),
            shape((group, lanes), BF),
            shape((group, width), BF),
            shape((group // 2, width), F32),
            shape((group // 2, width), BF),
        ),
        in_specs=[WHOLE] * 5 + [ANYWHERE] * (2 * len(own)),
        out_specs=(WHOLE,) * 5,
        scratch_shapes=planes_scratch(own),
        name="attend",
        cost_estimate=SHORT,
    )(x, docs[:, None], docs[None, :], cos, sin, *own, *oth)


def mlp_kernel(hat, cot, *refs):
    parts, refs = refs[:-11], refs[-11:]
    three, part, away, out_part, out_away, own, oth, sems, gate, upper, back = refs
    copies = load_planes(parts, own, oth, sems)
    begin(copies, range(3))
    cut = own.shape[1]
    count = part.shape[0]
    finish(copies, 0)
    gate[...] = nn(hat[:, :cut], own[0]) + nn(hat[:, cut:], oth[0])
    finish(copies, 1)
    upper[...] = nn(hat[:, :cut], own[1]) + nn(hat[:, cut:], oth[1])
    finish(copies, 2)
    back[...] = nn(cot[:, :cut], own[2]) + nn(cot[:, cut:], oth[2])
    step = 16

    def chunk(i, carry):
        at = pl.ds(pl.multiple_of(i * step, step), step)
        v, u, g = gate[at, :], upper[at, :], back[at, :]
        share = 0.5 * (1.0 + lax.erf(v * (1.0 / math.sqrt(2.0))))
        slope = share + v * (jnp.exp(-0.5 * v * v) * (1.0 / math.sqrt(2.0 * math.pi)))
        active = v * share
        three[0, at, :] = (g * u * slope).astype(BF)
        three[1, at, :] = (g * active).astype(BF)
        three[2, at, :] = (active * u).astype(BF)
        return carry

    lax.fori_loop(0, gate.shape[0] // step, chunk, 0)
    for weights, lo in ((own, 0), (oth, cut)):
        full = nt(three[0], weights[0]) + nt(three[1], weights[1])
        part[:, lo : lo + cut] = full[:count]
        away[:, lo : lo + cut] = full[count:].astype(BF)
        full = nt(three[2], weights[2])
        out_part[:, lo : lo + cut] = full[:count]
        out_away[:, lo : lo + cut] = full[count:].astype(BF)


def mlp_call(hat, cot, own, oth):
    group, width = hat.shape
    hidden = own[0].shape[2]
    half = group // 2
    return pl.pallas_call(
        mlp_kernel,
        out_shape=(
            shape((3, group, hidden), BF),
            shape((half, width), F32),
            shape((half, width), BF),
            shape((half, width), F32),
            shape((half, width), BF),
        ),
        in_specs=[WHOLE] * 2 + [ANYWHERE] * (2 * len(own)),
        out_specs=(WHOLE,) * 5,
        scratch_shapes=planes_scratch(own) + [pltpu.VMEM((group, hidden), F32)] * 3,
        name="mlp",
        cost_estimate=SHORT,
    )(hat, cot, *own, *oth)


def back_kernel(grad, qkv, docs, docs_row, cos, sin, *refs):
    parts, (three, part, away, own, oth, sems, gmix, wide) = refs[:-8], refs[-8:]
    copies = load_planes(parts, own, oth, sems)
    begin(copies, (3, 0, 1, 2))
    cut = own.shape[1]
    count = part.shape[0]
    finish(copies, 3)
    gmix[...] = (nn(grad[:, :cut], own[3]) + nn(grad[:, cut:], oth[3])).astype(BF)
    same = docs[...] == docs_row[...]
    for head in range(qkv.shape[2] // HDIM):
        at = slice(head * HDIM, (head + 1) * HDIM)
        query, key, value, outer = qkv[0, :, at], qkv[1, :, at], qkv[2, :, at], gmix[:, at]
        probs = head_probs(query, key, same)
        three[2, :, at] = tn(probs.astype(BF), outer).astype(BF)
        grad_probs = nt(outer, value)
        inner = jnp.sum(probs * grad_probs, axis=-1, keepdims=True)
        grad_scores = (probs * (grad_probs - inner) * 0.125).astype(BF)
        wide[0, :, at] = nn(grad_scores, key)
        wide[1, :, at] = tn(grad_scores, query)
    for plane in range(2):
        three[plane] = swing(wide[plane], cos[...], -sin[...]).astype(BF)
    for plane in range(3):
        finish(copies, plane)
    for weights, lo in ((own, 0), (oth, cut)):
        full = nt(three[0], weights[0]) + nt(three[1], weights[1]) + nt(three[2], weights[2])
        part[:, lo : lo + cut] = full[:count]
        away[:, lo : lo + cut] = full[count:].astype(BF)


def back_call(grad, qkv, own, oth, docs, cos, sin):
    group, width = grad.shape
    lanes = own[0].shape[2]
    return pl.pallas_call(
        back_kernel,
        out_shape=(
            shape((3, group, lanes), BF),
            shape((group // 2, width), F32),
            shape((group // 2, width), BF),
        ),
        in_specs=[WHOLE] * 6 + [ANYWHERE] * (2 * len(own)),
        out_specs=(WHOLE,) * 3,
        scratch_shapes=planes_scratch(own)
        + [pltpu.VMEM((group, lanes), BF), pltpu.VMEM((2, group, lanes), F32)],
        name="attend_back",
        cost_estimate=SHORT,
    )(grad, qkv, docs[:, None], docs[None, :], cos, sin, *own, *oth)


def outer_kernel(first, second, three, last, out, turned):
    plane = pl.program_id(0)
    split = pl.num_programs(0) - 1

    @pl.when(plane == 0)
    def _():
        turned[...] = first[...].T

    @pl.when(plane == split)
    def _():
        turned[...] = second[...].T

    @pl.when(plane < split)
    def _():
        out[0] = nn(turned[...], three[0]).astype(BF)

    @pl.when(plane == split)
    def _():
        out[0] = nn(turned[...], last[...]).astype(BF)


def weight_grads(first, second, three, last, side):
    group, width = first.shape
    cut = width // 2
    lanes = three.shape[2]
    merged = last is None
    planes = 3 if merged else 4
    last_spec = pl.BlockSpec((group, lanes), lambda i: (0, 0))
    if merged:
        last = three
        last_spec = pl.BlockSpec((None, group, lanes), lambda i: (2, 0, 0))
    return pl.pallas_call(
        outer_kernel,
        grid=(planes,),
        out_shape=shape((planes, cut, lanes), BF),
        in_specs=[
            pl.BlockSpec((group, cut), lambda i: (0, side)),
            pl.BlockSpec((group, cut), lambda i: (0, side)),
            pl.BlockSpec((1, group, lanes), lambda i: (jnp.minimum(i, planes - 2), 0, 0)),
            last_spec,
        ],
        out_specs=pl.BlockSpec((1, cut, lanes), lambda i: (i, 0, 0)),
        scratch_shapes=[pltpu.VMEM((cut, group), BF)],
        name="weight_grads",
        cost_estimate=LONG,
    )(first, second, three, last)


def ring_sum(name, own, theirs, got, j, count, outs, compute):
    planes, _, lanes = own.shape
    near = theirs.size <= NEAR
    n_got, n_out = len(got), len(outs)
    n_far = 1 if near else 2

    def kernel(*refs):
        sources = refs[:2]
        received = refs[2 : 2 + n_got]
        made = refs[2 + n_got : 2 + n_got + n_out]
        held = refs[2 + n_got + n_out : -1]
        sems = refs[-1]
        copies = []
        for plane in range(planes):
            copies.append(
                [
                    pltpu.make_async_copy(
                        sources[k].at[plane, pl.ds(j, count)], held[k].at[plane], sems.at[k, plane]
                    )
                    for k in range(n_far)
                ]
            )
            for copy in copies[plane]:
                copy.start()
        for plane in range(planes):
            for copy in copies[plane]:
                copy.wait()
            second = sources[1][plane, j : j + count] if near else held[1][plane]
            total = held[0][plane].astype(F32) + second.astype(F32)
            compute(total, [r[plane].astype(F32) for r in received], [m.at[plane] for m in made])

    return pl.pallas_call(
        kernel,
        out_shape=tuple(shape((planes, r, lanes), kind) for r, kind in outs),
        in_specs=[ANYWHERE, WHOLE if near else ANYWHERE] + [WHOLE] * n_got,
        out_specs=(WHOLE,) * n_out,
        scratch_shapes=[pltpu.VMEM((planes, count, lanes), BF)] * n_far
        + [pltpu.SemaphoreType.DMA((n_far, planes))],
        name=name,
        cost_estimate=SHORT,
    )(own, theirs, *got)


def first_call(own, theirs, rows, j):
    h = rows // 2

    def compute(total, got, made):
        made[0][...] = total[:h].astype(BF)
        made[1][...] = total[h:].astype(BF)

    return ring_sum("ring_first", own, theirs, (), j * rows, rows, ((h, BF), (h, BF)), compute)


def middle_call(own, theirs, down, up, rows, j):
    h = down.shape[1]

    def compute(total, got, made):
        a, b = total[:rows], total[rows:]
        made[0][:h] = (a[:h] + got[0]).astype(BF)
        made[1][rows - h :] = (b[rows - h :] + got[1]).astype(BF)
        if h < rows:
            made[0][h:] = a[h:].astype(BF)
            made[1][: rows - h] = b[: rows - h].astype(BF)

    return ring_sum(
        "ring_middle", own, theirs, (down, up), j * rows, 2 * rows, ((rows, BF), (rows, BF)), compute
    )


def last_call(own, theirs, down, up, rows):
    def compute(total, got, made):
        made[0][...] = total + (got[0] + got[1])

    return ring_sum("ring_last", own, theirs, (down, up), 0, rows, ((rows, F32),), compute)[0]


def close(value):
    return pltpu.with_memory_space_constraint(value, pltpu.VMEM)


def tie(value, *after):
    return lax.optimization_barrier((value, after))[0]


class Ring:
    def __init__(self, size):
        self.size = size
        self.chips = size // 2
        self.ringed = self.chips % 2 == 0 and 4 <= self.chips <= 16
        half = self.chips // 2
        order = [2 * p for p in range(half)] + [2 * (self.chips - 1 - p) + 1 for p in range(half, self.chips)]
        self.forward = self.pairs(order, 1)
        self.backward = self.pairs(order, -1)
        self.core = [(i, i ^ 1) for i in range(size)]
        self.groups = [[i for i in range(size) if i % 2 == c] for c in range(2)]

    def pairs(self, order, step):
        n = self.chips
        return [
            (2 * order[k] + c, 2 * order[(k + step) % n] + c) for k in range(n) for c in range(2)
        ]

    def arrival(self, rows):
        me = lax.axis_index("dp")
        chip, core = me // 2, me % 2
        n, half = self.chips, self.chips // 2
        place = jnp.arange(self.size * rows, dtype=jnp.int32)
        other = place // (n * rows)
        block = (place // rows) % n
        if self.ringed:
            spot = jnp.where(chip % 2 == 0, chip // 2, n - 1 - chip // 2)
            offset = jnp.where(block % 2 == 1, -((block + 1) // 2), block // 2)
            where_at = (spot + offset + n) % n
            source = jnp.where(where_at < half, 2 * where_at, 2 * (n - 1 - where_at) + 1)
        else:
            source = block
        return (source * 2 + (core + other) % 2) * rows + place % rows

    def ahead(self, block):
        return lax.ppermute(block, "dp", self.forward)

    def back(self, block):
        return lax.ppermute(block, "dp", self.backward)

    def across(self, block):
        return lax.ppermute(block, "dp", self.core)


class Gather:
    def __init__(self, ring, block):
        self.ring = ring
        self.block = block
        self.pieces = [block]
        self.a = self.b = block
        self.left = ring.chips // 2 if ring.ringed else 0
        self.kept = ring.chips - 3

    def step(self, *after):
        if self.left == 0:
            return
        a, b = (tie((self.a, self.b), *after) if after else (self.a, self.b))
        self.left -= 1
        if self.left == 0:
            rows = a.shape[1]
            a, b = a[:, : rows // 2], b[:, rows // 2 :]
        self.a, self.b = self.ring.ahead(a), self.ring.back(b)
        self.pieces += [self.a, self.b]

    def early(self, *after):
        if not self.ring.ringed:
            return
        part = stack_call([tie(self.pieces[0], *after)] + self.pieces[1 : self.kept], 1)
        self.parts = [(part, self.ring.across(part))]
        self.pieces = self.pieces[self.kept :]

    def done(self):
        if self.ring.ringed:
            part = stack_call(self.pieces[-4:], 0)
            self.parts.append((part, self.ring.across(part)))
        else:
            part = lax.all_gather(
                self.block, "dp", axis=1, tiled=True, axis_index_groups=self.ring.groups
            )
            self.parts = [(part, self.ring.across(part))]
        return tuple(zip(*self.parts))


class Reduce:
    def __init__(self, ring, own, theirs):
        near = ring.ringed and theirs.size <= NEAR
        self.ring, self.own, self.theirs = ring, own, close(theirs) if near else theirs
        self.rows = own.shape[1] // ring.chips
        self.left = ring.chips // 2 if ring.ringed else 0
        self.down = self.up = None
        self.sent = ()

    def step(self, *after):
        if self.left == 0:
            return
        j = 2 * self.left - 1
        if self.down is None:
            down, up = first_call(self.own, self.theirs, self.rows, j)
        else:
            down, up = middle_call(self.own, self.theirs, self.down, self.up, self.rows, j)
        if after:
            down, up = tie((down, up), *after)
        self.left -= 1
        self.sent = (down, up)
        self.down, self.up = close(self.ring.back(down)), close(self.ring.ahead(up))

    def done(self, *after):
        if not self.ring.ringed:
            total = self.own.astype(F32) + self.theirs.astype(F32)
            return lax.psum_scatter(
                total, "dp", scatter_dimension=1, tiled=True, axis_index_groups=self.ring.groups
            )
        own = tie(self.own, *after) if after else self.own
        return last_call(own, self.theirs, self.down, self.up, self.rows)


def swap(block):
    return lax.ppermute(block, "tensor", [(0, 1), (1, 0)])


def body(tokens, seq_lens, g_attn, w_qkv, w_ao, g_mlp, w_in, w_mo, cotangent):
    ring = Ring(lax.axis_size("dp"))
    rows = w_qkv.shape[0]
    count = tokens.shape[0]
    side = lax.axis_index("tensor")
    group = 2 * count
    width = tokens.shape[1]

    gain_one = g_attn.astype(F32)
    gain_two = g_mlp.astype(F32)
    plain_qkv = jnp.transpose(w_qkv, (1, 0, 2)).astype(F32)
    plain_in = jnp.transpose(w_in, (1, 0, 2)).astype(F32)
    block_a = jnp.concatenate(
        [(plain_qkv * gain_one[None, :, None]).astype(BF), w_ao.T[None]], axis=0
    )
    hidden = w_in.shape[2]
    block_b = jnp.concatenate(
        [(plain_in * gain_two[None, :, None]).astype(BF), w_mo.T[None]], axis=0
    )
    block_b = jnp.pad(block_b, ((0, 0), (0, 0), (0, -hidden % 128)))
    gather_a = Gather(ring, block_a)
    gather_a.step()
    gather_b = Gather(ring, tie(block_b, block_a))
    gather_b.step()

    index = (jnp.arange(group, dtype=jnp.int32) + side * count) % group
    docs, positions = layout(seq_lens[0], index)
    cosine, sine = tables(positions, w_qkv.shape[2])

    places = ring.arrival(rows)
    chosen = (jnp.arange(width, dtype=jnp.int32)[:, None] == places[None, :]).astype(BF)
    moved = ein("td,de->te", jnp.concatenate([tokens, cotangent], axis=0), chosen).astype(BF)
    moved_other = swap(moved)
    tokens_all = jnp.concatenate([moved[:count], moved_other[:count]], axis=0)
    cot_all = jnp.concatenate([moved[count:], moved_other[count:]], axis=0)

    gather_a.step(moved)
    gather_a.early()
    gather_a.step(cosine, sine)
    gather_a.step(tokens_all, cot_all, gather_b.a, gather_b.b)
    gather_b.step(*gather_a.pieces[:2])
    own_a, oth_a = gather_a.done()

    normed_one, factor_one = normalize(moved[:count].astype(F32))
    qkv, mixed, hat_one, part, away = attend_call(tokens_all, own_a, oth_a, docs, cosine, sine)
    swapped = swap(away)
    gather_b.step(away)
    residual = moved[:count].astype(F32) + part + swapped.astype(F32)
    normed_two, factor_two = normalize(residual)
    hat_own = normed_two.astype(BF)
    gather_b.early(hat_own)
    hat_two = jnp.concatenate([hat_own, swap(hat_own)], axis=0)
    gather_b.step(hat_two)
    own_b, oth_b = gather_b.done()

    three_b, part, away, out_part, out_away = mlp_call(hat_two, cot_all, own_b, oth_b)
    swapped = swap(away)
    side_b = weight_grads(hat_two, cot_all, three_b, None, 1)
    cross_b = ring.across(side_b)
    main_b = weight_grads(tie(hat_two, side_b), cot_all, three_b, None, 0)
    reduce_b = Reduce(ring, main_b, cross_b)
    reduce_b.step()
    grad_hat_two = part + tie(swapped, *reduce_b.sent).astype(F32)
    grad_residual = moved[count:].astype(F32) + norm_back(grad_hat_two, normed_two, factor_two)
    grad_res_own = grad_residual.astype(BF)
    grad_res_all = jnp.concatenate([grad_res_own, swap(grad_res_own)], axis=0)
    reduce_b.step(grad_res_all)
    three_a, part, away = back_call(
        tie(grad_res_all, *reduce_b.sent), qkv, own_a, oth_a, docs, cosine, sine
    )
    reduce_b.step(away)
    swapped = swap(away)
    side_a = weight_grads(tie(hat_one, *reduce_b.sent), grad_res_all, three_a, mixed, 1)
    cross_a = ring.across(side_a)
    main_a = weight_grads(tie(hat_one, side_a), grad_res_all, three_a, mixed, 0)
    reduce_a = Reduce(ring, main_a, cross_a)
    reduce_a.step()
    reduce_b.step(*reduce_a.sent)
    reduce_a.step(*reduce_b.sent)
    raw_b = reduce_b.done(*reduce_a.sent)

    grad_hat_one = part + tie(swapped, *reduce_a.sent).astype(F32)
    grad_input = grad_residual + norm_back(grad_hat_one, normed_one, factor_one)
    top = lax.reduce_precision(grad_input, 8, 7)
    middle = lax.reduce_precision(grad_input - top, 8, 7)
    parts = jnp.concatenate([top, middle, grad_input - top - middle], axis=0).astype(BF)
    spread = ein("te,de->td", parts, chosen)
    grad_input = spread[:count] + spread[count : 2 * count] + spread[2 * count :]
    out_swapped = swap(tie(out_away, swapped))
    reduce_a.step(grad_input)

    raw_b = tie(raw_b, *reduce_a.sent)[:, :, :hidden]
    grad_in = jnp.transpose(raw_b[:2] * gain_two[None, :, None], (1, 0, 2))
    grad_mo = raw_b[2].T
    gain_two_sum = jnp.sum(plain_in * raw_b[:2], axis=(0, 2))
    reduce_a.step(grad_in, grad_mo, gain_two_sum)
    output = (residual + out_part + tie(out_swapped, *reduce_a.sent).astype(F32)).astype(BF)
    output = ein("te,de->td", output, chosen).astype(BF)
    raw_a = reduce_a.done()

    gain_sums = jnp.stack(
        [jnp.sum(plain_qkv * raw_a[:3], axis=(0, 2)), gain_two_sum]
    )
    share = rows // 2
    gain_shares = lax.dynamic_slice_in_dim(gain_sums, side * share, share, 1) + swap(
        lax.dynamic_slice_in_dim(gain_sums, (1 - side) * share, share, 1)
    )
    return (
        output,
        grad_input,
        gain_shares[0],
        jnp.transpose(raw_a[:3] * gain_one[None, :, None], (1, 0, 2)),
        raw_a[3].T,
        gain_shares[1],
        grad_in,
        grad_mo,
    )


def solution(mesh):
    return jax.shard_map(
        body,
        mesh=mesh,
        in_specs=(
            P(("dp", "tensor"), None),
            P("dp", None),
            P("dp"),
            P("dp", None, "tensor"),
            P("tensor", "dp"),
            P("dp"),
            P("dp", None, "tensor"),
            P("tensor", "dp"),
            P(("dp", "tensor"), None),
        ),
        out_specs=(
            P(("dp", "tensor"), None),
            P(("dp", "tensor"), None),
            P(("dp", "tensor")),
            P("dp", None, "tensor"),
            P("tensor", "dp"),
            P(("dp", "tensor")),
            P("dp", None, "tensor"),
            P("tensor", "dp"),
        ),
        check_vma=False,
    )
```

```python
import math

import jax
import jax.numpy as jnp
from jax import lax
from jax.experimental import pallas as pl
from jax.experimental.pallas import tpu as pltpu
from jax.sharding import PartitionSpec as P

HDIM = 64
ROPE_BASE = 160000.0
BF = jnp.bfloat16
F32 = jnp.float32


def layout(lengths, index):
    ends = jnp.cumsum(lengths)
    passed = ends[None, :] <= index[:, None]
    doc_ids = jnp.sum(passed.astype(jnp.int32), axis=1)
    begins = jnp.max(jnp.where(passed, ends[None, :], jnp.zeros_like(ends)[None, :]), axis=1)
    return (doc_ids, index - begins)


def tables(positions, lanes):
    half = HDIM // 2
    lane = jnp.arange(lanes, dtype=jnp.int32)
    rates = jnp.exp((lane % half).astype(F32) * (-2.0 * math.log(ROPE_BASE) / HDIM))
    angles = positions.astype(F32)[:, None] * rates[None, :]
    sign = jnp.where(lane % HDIM < half, -1.0, 1.0)
    return jnp.cos(angles), jnp.sin(angles) * sign[None, :]


def normalize(values):
    center = values - jnp.mean(values, axis=-1, keepdims=True)
    factor = lax.rsqrt(jnp.mean(center * center, axis=-1, keepdims=True) + 1e-05)
    return (center * factor, factor)


def norm_back(grad_hat, normed, factor):
    return factor * (
        grad_hat
        - jnp.mean(grad_hat, axis=-1, keepdims=True)
        - normed * jnp.mean(grad_hat * normed, axis=-1, keepdims=True)
    )


def ein(spec, left, right):
    return jnp.einsum(spec, left, right, preferred_element_type=F32)


def nn(left, right):
    return jnp.dot(left, right, preferred_element_type=F32)


def nt(left, right):
    return lax.dot_general(left, right, (((1,), (1,)), ((), ())), preferred_element_type=F32)


def tn(left, right):
    return lax.dot_general(left, right, (((0,), (0,)), ((), ())), preferred_element_type=F32)


def shape(dims, kind):
    return jax.ShapeDtypeStruct(dims, kind)


ANYWHERE = pl.BlockSpec(memory_space=pltpu.HBM)
LONG = pl.CostEstimate(flops=10**11, bytes_accessed=10**9, transcendentals=0)
NEAR = 2**20
SHORT = pl.CostEstimate(flops=1000, bytes_accessed=1000, transcendentals=0)
WHOLE = pl.BlockSpec(memory_space=pltpu.VMEM)


def load_planes(parts, own, oth, sems):
    half = len(parts) // 2
    copies = []
    for plane in range(own.shape[0]):
        copies.append([])
        for k, part in enumerate(parts):
            at = sum(q.shape[1] for q in parts[k // half * half : k])
            target = (own if k < half else oth).at[plane, pl.ds(at, part.shape[1])]
            copies[plane].append(pltpu.make_async_copy(part.at[plane], target, sems.at[k, plane]))
    return copies


def begin(copies, order):
    for plane in order:
        for copy in copies[plane]:
            copy.start()


def finish(copies, plane):
    for copy in copies[plane]:
        copy.wait()


def held_block(own):
    return (own[0].shape[0], sum(part.shape[1] for part in own), own[0].shape[2])


def planes_scratch(own):
    block = held_block(own)
    return [
        pltpu.VMEM(block, BF),
        pltpu.VMEM(block, BF),
        pltpu.SemaphoreType.DMA((2 * len(own), block[0])),
    ]


def stack_kernel(*refs):
    pieces, out, sems = refs[:-2], refs[-2], refs[-1]
    copies, at = [], 0
    for k, piece in enumerate(pieces):
        copies.append(
            pltpu.make_async_copy(piece, out.at[:, pl.ds(at, piece.shape[1])], sems.at[k])
        )
        copies[k].start()
        at += piece.shape[1]
    for copy in copies:
        copy.wait()


def stack_call(pieces, far):
    planes, _, lanes = pieces[0].shape
    return pl.pallas_call(
        stack_kernel,
        out_shape=shape((planes, sum(p.shape[1] for p in pieces), lanes), BF),
        in_specs=[WHOLE] * len(pieces),
        out_specs=ANYWHERE,
        scratch_shapes=[pltpu.SemaphoreType.DMA((len(pieces),))],
        name="stack_rows",
        cost_estimate=LONG,
    )(*pieces[:far], *[close(piece) for piece in pieces[far:]])


def swing(values, cosine, sine):
    lanes = values.shape[-1]
    half = HDIM // 2
    lane = lax.broadcasted_iota(jnp.int32, values.shape, 1)
    turned = jnp.where(
        lane % HDIM < half,
        pltpu.roll(values, lanes - half, 1),
        pltpu.roll(values, half, 1),
    )
    return values * cosine + turned * sine


def head_probs(query, key, same):
    scores = jnp.where(same, nt(query, key) * 0.125, -1e30)
    peak = jnp.max(scores, axis=-1, keepdims=True)
    raised = jnp.exp(scores - peak)
    return raised * (1.0 / jnp.sum(raised, axis=-1, keepdims=True))


def attend_kernel(x, docs, docs_row, cos, sin, *refs):
    parts, (qkv, mixed, hat, part, away, own, oth, sems) = refs[:-8], refs[-8:]
    copies = load_planes(parts, own, oth, sems)
    begin(copies, range(4))
    normed, _ = normalize(x[...].astype(F32))
    hat[...] = normed.astype(BF)
    cut = own.shape[1]
    count = part.shape[0]
    for plane in range(3):
        finish(copies, plane)
        value = nn(hat[:, :cut], own[plane]) + nn(hat[:, cut:], oth[plane])
        if plane < 2:
            value = swing(value, cos[...], sin[...])
        qkv[plane] = value.astype(BF)
    same = docs[...] == docs_row[...]
    for head in range(qkv.shape[2] // HDIM):
        at = slice(head * HDIM, (head + 1) * HDIM)
        probs = head_probs(qkv[0, :, at], qkv[1, :, at], same)
        mixed[:, at] = nn(probs.astype(BF), qkv[2, :, at]).astype(BF)
    finish(copies, 3)
    for weights, lo in ((own, 0), (oth, cut)):
        full = nt(mixed[...], weights[3])
        part[:, lo : lo + cut] = full[:count]
        away[:, lo : lo + cut] = full[count:].astype(BF)


def attend_call(x, own, oth, docs, cos, sin):
    group, width = x.shape
    lanes = own[0].shape[2]
    return pl.pallas_call(
        attend_kernel,
        out_shape=(
            shape((3, group, lanes), BF),
            shape((group, lanes), BF),
            shape((group, width), BF),
            shape((group // 2, width), F32),
            shape((group // 2, width), BF),
        ),
        in_specs=[WHOLE] * 5 + [ANYWHERE] * (2 * len(own)),
        out_specs=(WHOLE,) * 5,
        scratch_shapes=planes_scratch(own),
        name="attend",
        cost_estimate=SHORT,
    )(x, docs[:, None], docs[None, :], cos, sin, *own, *oth)


def mlp_kernel(hat, cot, *refs):
    parts, refs = refs[:-11], refs[-11:]
    three, part, away, out_part, out_away, own, oth, sems, gate, upper, back = refs
    copies = load_planes(parts, own, oth, sems)
    begin(copies, range(3))
    cut = own.shape[1]
    count = part.shape[0]
    finish(copies, 0)
    gate[...] = nn(hat[:, :cut], own[0]) + nn(hat[:, cut:], oth[0])
    finish(copies, 1)
    upper[...] = nn(hat[:, :cut], own[1]) + nn(hat[:, cut:], oth[1])
    finish(copies, 2)
    back[...] = nn(cot[:, :cut], own[2]) + nn(cot[:, cut:], oth[2])
    step = 16

    def chunk(i, carry):
        at = pl.ds(pl.multiple_of(i * step, step), step)
        v, u, g = gate[at, :], upper[at, :], back[at, :]
        share = 0.5 * (1.0 + lax.erf(v * (1.0 / math.sqrt(2.0))))
        slope = share + v * (jnp.exp(-0.5 * v * v) * (1.0 / math.sqrt(2.0 * math.pi)))
        active = v * share
        three[0, at, :] = (g * u * slope).astype(BF)
        three[1, at, :] = (g * active).astype(BF)
        three[2, at, :] = (active * u).astype(BF)
        return carry

    lax.fori_loop(0, gate.shape[0] // step, chunk, 0)
    for weights, lo in ((own, 0), (oth, cut)):
        full = nt(three[0], weights[0]) + nt(three[1], weights[1])
        part[:, lo : lo + cut] = full[:count]
        away[:, lo : lo + cut] = full[count:].astype(BF)
        full = nt(three[2], weights[2])
        out_part[:, lo : lo + cut] = full[:count]
        out_away[:, lo : lo + cut] = full[count:].astype(BF)


def mlp_call(hat, cot, own, oth):
    group, width = hat.shape
    hidden = own[0].shape[2]
    half = group // 2
    return pl.pallas_call(
        mlp_kernel,
        out_shape=(
            shape((3, group, hidden), BF),
            shape((half, width), F32),
            shape((half, width), BF),
            shape((half, width), F32),
            shape((half, width), BF),
        ),
        in_specs=[WHOLE] * 2 + [ANYWHERE] * (2 * len(own)),
        out_specs=(WHOLE,) * 5,
        scratch_shapes=planes_scratch(own) + [pltpu.VMEM((group, hidden), F32)] * 3,
        name="mlp",
        cost_estimate=SHORT,
    )(hat, cot, *own, *oth)


def back_kernel(grad, qkv, docs, docs_row, cos, sin, *refs):
    parts, (three, part, away, own, oth, sems, gmix, wide) = refs[:-8], refs[-8:]
    copies = load_planes(parts, own, oth, sems)
    begin(copies, (3, 0, 1, 2))
    cut = own.shape[1]
    count = part.shape[0]
    finish(copies, 3)
    gmix[...] = (nn(grad[:, :cut], own[3]) + nn(grad[:, cut:], oth[3])).astype(BF)
    same = docs[...] == docs_row[...]
    for head in range(qkv.shape[2] // HDIM):
        at = slice(head * HDIM, (head + 1) * HDIM)
        query, key, value, outer = qkv[0, :, at], qkv[1, :, at], qkv[2, :, at], gmix[:, at]
        probs = head_probs(query, key, same)
        three[2, :, at] = tn(probs.astype(BF), outer).astype(BF)
        grad_probs = nt(outer, value)
        inner = jnp.sum(probs * grad_probs, axis=-1, keepdims=True)
        grad_scores = (probs * (grad_probs - inner) * 0.125).astype(BF)
        wide[0, :, at] = nn(grad_scores, key)
        wide[1, :, at] = tn(grad_scores, query)
    for plane in range(2):
        three[plane] = swing(wide[plane], cos[...], -sin[...]).astype(BF)
    for plane in range(3):
        finish(copies, plane)
    for weights, lo in ((own, 0), (oth, cut)):
        full = nt(three[0], weights[0]) + nt(three[1], weights[1]) + nt(three[2], weights[2])
        part[:, lo : lo + cut] = full[:count]
        away[:, lo : lo + cut] = full[count:].astype(BF)


def back_call(grad, qkv, own, oth, docs, cos, sin):
    group, width = grad.shape
    lanes = own[0].shape[2]
    return pl.pallas_call(
        back_kernel,
        out_shape=(
            shape((3, group, lanes), BF),
            shape((group // 2, width), F32),
            shape((group // 2, width), BF),
        ),
        in_specs=[WHOLE] * 6 + [ANYWHERE] * (2 * len(own)),
        out_specs=(WHOLE,) * 3,
        scratch_shapes=planes_scratch(own)
        + [pltpu.VMEM((group, lanes), BF), pltpu.VMEM((2, group, lanes), F32)],
        name="attend_back",
        cost_estimate=SHORT,
    )(grad, qkv, docs[:, None], docs[None, :], cos, sin, *own, *oth)


def outer_kernel(first, second, three, last, out, turned):
    plane = pl.program_id(0)
    split = pl.num_programs(0) - 1

    @pl.when(plane == 0)
    def _():
        turned[...] = first[...].T

    @pl.when(plane == split)
    def _():
        turned[...] = second[...].T

    @pl.when(plane < split)
    def _():
        out[0] = nn(turned[...], three[0]).astype(BF)

    @pl.when(plane == split)
    def _():
        out[0] = nn(turned[...], last[...]).astype(BF)


def weight_grads(first, second, three, last, side):
    group, width = first.shape
    cut = width // 2
    lanes = three.shape[2]
    merged = last is None
    planes = 3 if merged else 4
    last_spec = pl.BlockSpec((group, lanes), lambda i: (0, 0))
    if merged:
        last = three
        last_spec = pl.BlockSpec((None, group, lanes), lambda i: (2, 0, 0))
    return pl.pallas_call(
        outer_kernel,
        grid=(planes,),
        out_shape=shape((planes, cut, lanes), BF),
        in_specs=[
            pl.BlockSpec((group, cut), lambda i: (0, side)),
            pl.BlockSpec((group, cut), lambda i: (0, side)),
            pl.BlockSpec((1, group, lanes), lambda i: (jnp.minimum(i, planes - 2), 0, 0)),
            last_spec,
        ],
        out_specs=pl.BlockSpec((1, cut, lanes), lambda i: (i, 0, 0)),
        scratch_shapes=[pltpu.VMEM((cut, group), BF)],
        name="weight_grads",
        cost_estimate=LONG,
    )(first, second, three, last)


def ring_sum(name, own, theirs, got, j, count, outs, compute):
    planes, _, lanes = own.shape
    near = theirs.size <= NEAR
    n_got, n_out = len(got), len(outs)
    n_far = 1 if near else 2

    def kernel(*refs):
        sources = refs[:2]
        received = refs[2 : 2 + n_got]
        made = refs[2 + n_got : 2 + n_got + n_out]
        held = refs[2 + n_got + n_out : -1]
        sems = refs[-1]
        copies = []
        for plane in range(planes):
            copies.append(
                [
                    pltpu.make_async_copy(
                        sources[k].at[plane, pl.ds(j, count)], held[k].at[plane], sems.at[k, plane]
                    )
                    for k in range(n_far)
                ]
            )
            for copy in copies[plane]:
                copy.start()
        for plane in range(planes):
            for copy in copies[plane]:
                copy.wait()
            second = sources[1][plane, j : j + count] if near else held[1][plane]
            total = held[0][plane].astype(F32) + second.astype(F32)
            compute(total, [r[plane].astype(F32) for r in received], [m.at[plane] for m in made])

    return pl.pallas_call(
        kernel,
        out_shape=tuple(shape((planes, r, lanes), kind) for r, kind in outs),
        in_specs=[ANYWHERE, WHOLE if near else ANYWHERE] + [WHOLE] * n_got,
        out_specs=(WHOLE,) * n_out,
        scratch_shapes=[pltpu.VMEM((planes, count, lanes), BF)] * n_far
        + [pltpu.SemaphoreType.DMA((n_far, planes))],
        name=name,
        cost_estimate=SHORT,
    )(own, theirs, *got)


def first_call(own, theirs, rows, j):
    h = rows // 2

    def compute(total, got, made):
        made[0][...] = total[:h].astype(BF)
        made[1][...] = total[h:].astype(BF)

    return ring_sum("ring_first", own, theirs, (), j * rows, rows, ((h, BF), (h, BF)), compute)


def middle_call(own, theirs, down, up, rows, j):
    h = down.shape[1]

    def compute(total, got, made):
        a, b = total[:rows], total[rows:]
        made[0][:h] = (a[:h] + got[0]).astype(BF)
        made[1][rows - h :] = (b[rows - h :] + got[1]).astype(BF)
        if h < rows:
            made[0][h:] = a[h:].astype(BF)
            made[1][: rows - h] = b[: rows - h].astype(BF)

    return ring_sum(
        "ring_middle", own, theirs, (down, up), j * rows, 2 * rows, ((rows, BF), (rows, BF)), compute
    )


def last_call(own, theirs, down, up, rows):
    def compute(total, got, made):
        made[0][...] = total + (got[0] + got[1])

    return ring_sum("ring_last", own, theirs, (down, up), 0, rows, ((rows, F32),), compute)[0]


def close(value):
    return pltpu.with_memory_space_constraint(value, pltpu.VMEM)


def tie(value, *after):
    return lax.optimization_barrier((value, after))[0]


class Ring:
    def __init__(self, size):
        self.size = size
        self.chips = size // 2
        self.ringed = self.chips % 2 == 0 and 4 <= self.chips <= 16
        half = self.chips // 2
        order = [2 * p for p in range(half)] + [2 * (self.chips - 1 - p) + 1 for p in range(half, self.chips)]
        self.forward = self.pairs(order, 1)
        self.backward = self.pairs(order, -1)
        self.core = [(i, i ^ 1) for i in range(size)]
        self.groups = [[i for i in range(size) if i % 2 == c] for c in range(2)]

    def pairs(self, order, step):
        n = self.chips
        return [
            (2 * order[k] + c, 2 * order[(k + step) % n] + c) for k in range(n) for c in range(2)
        ]

    def arrival(self, rows):
        me = lax.axis_index("dp")
        chip, core = me // 2, me % 2
        n, half = self.chips, self.chips // 2
        place = jnp.arange(self.size * rows, dtype=jnp.int32)
        other = place // (n * rows)
        block = (place // rows) % n
        if self.ringed:
            spot = jnp.where(chip % 2 == 0, chip // 2, n - 1 - chip // 2)
            offset = jnp.where(block % 2 == 1, -((block + 1) // 2), block // 2)
            where_at = (spot + offset + n) % n
            source = jnp.where(where_at < half, 2 * where_at, 2 * (n - 1 - where_at) + 1)
        else:
            source = block
        return (source * 2 + (core + other) % 2) * rows + place % rows

    def ahead(self, block):
        return lax.ppermute(block, "dp", self.forward)

    def back(self, block):
        return lax.ppermute(block, "dp", self.backward)

    def across(self, block):
        return lax.ppermute(block, "dp", self.core)


class Gather:
    def __init__(self, ring, block):
        self.ring = ring
        self.block = block
        self.pieces = [block]
        self.a = self.b = block
        self.left = ring.chips // 2 if ring.ringed else 0
        self.kept = ring.chips - 3

    def step(self, *after):
        if self.left == 0:
            return
        a, b = (tie((self.a, self.b), *after) if after else (self.a, self.b))
        self.left -= 1
        if self.left == 0:
            rows = a.shape[1]
            a, b = a[:, : rows // 2], b[:, rows // 2 :]
        self.a, self.b = self.ring.ahead(a), self.ring.back(b)
        self.pieces += [self.a, self.b]

    def early(self, *after):
        if not self.ring.ringed:
            return
        part = stack_call([tie(self.pieces[0], *after)] + self.pieces[1 : self.kept], 1)
        self.parts = [(part, self.ring.across(part))]
        self.pieces = self.pieces[self.kept :]

    def done(self):
        if self.ring.ringed:
            part = stack_call(self.pieces[-4:], 0)
            self.parts.append((part, self.ring.across(part)))
        else:
            part = lax.all_gather(
                self.block, "dp", axis=1, tiled=True, axis_index_groups=self.ring.groups
            )
            self.parts = [(part, self.ring.across(part))]
        return tuple(zip(*self.parts))


class Reduce:
    def __init__(self, ring, own, theirs):
        near = ring.ringed and theirs.size <= NEAR
        self.ring, self.own, self.theirs = ring, own, close(theirs) if near else theirs
        self.rows = own.shape[1] // ring.chips
        self.left = ring.chips // 2 if ring.ringed else 0
        self.down = self.up = None
        self.sent = ()

    def step(self, *after):
        if self.left == 0:
            return
        j = 2 * self.left - 1
        if self.down is None:
            down, up = first_call(self.own, self.theirs, self.rows, j)
        else:
            down, up = middle_call(self.own, self.theirs, self.down, self.up, self.rows, j)
        if after:
            down, up = tie((down, up), *after)
        self.left -= 1
        self.sent = (down, up)
        self.down, self.up = close(self.ring.back(down)), close(self.ring.ahead(up))

    def done(self, *after):
        if not self.ring.ringed:
            total = self.own.astype(F32) + self.theirs.astype(F32)
            return lax.psum_scatter(
                total, "dp", scatter_dimension=1, tiled=True, axis_index_groups=self.ring.groups
            )
        own = tie(self.own, *after) if after else self.own
        return last_call(own, self.theirs, self.down, self.up, self.rows)


def swap(block):
    return lax.ppermute(block, "tensor", [(0, 1), (1, 0)])


def body(tokens, seq_lens, g_attn, w_qkv, w_ao, g_mlp, w_in, w_mo, cotangent):
    ring = Ring(lax.axis_size("dp"))
    rows = w_qkv.shape[0]
    count = tokens.shape[0]
    side = lax.axis_index("tensor")
    group = 2 * count
    width = tokens.shape[1]

    gain_one = g_attn.astype(F32)
    gain_two = g_mlp.astype(F32)
    plain_qkv = jnp.transpose(w_qkv, (1, 0, 2)).astype(F32)
    plain_in = jnp.transpose(w_in, (1, 0, 2)).astype(F32)
    block_a = jnp.concatenate(
        [(plain_qkv * gain_one[None, :, None]).astype(BF), w_ao.T[None]], axis=0
    )
    hidden = w_in.shape[2]
    block_b = jnp.concatenate(
        [(plain_in * gain_two[None, :, None]).astype(BF), w_mo.T[None]], axis=0
    )
    block_b = jnp.pad(block_b, ((0, 0), (0, 0), (0, -hidden % 128)))
    gather_a = Gather(ring, block_a)
    gather_a.step()
    gather_b = Gather(ring, tie(block_b, block_a))
    gather_b.step()

    index = (jnp.arange(group, dtype=jnp.int32) + side * count) % group
    docs, positions = layout(seq_lens[0], index)
    cosine, sine = tables(positions, w_qkv.shape[2])

    places = ring.arrival(rows)
    chosen = (jnp.arange(width, dtype=jnp.int32)[:, None] == places[None, :]).astype(BF)
    moved = ein("td,de->te", jnp.concatenate([tokens, cotangent], axis=0), chosen).astype(BF)
    moved_other = swap(moved)
    tokens_all = jnp.concatenate([moved[:count], moved_other[:count]], axis=0)
    cot_all = jnp.concatenate([moved[count:], moved_other[count:]], axis=0)

    gather_a.step(moved)
    gather_a.early()
    gather_a.step(cosine, sine)
    gather_a.step(tokens_all, cot_all, gather_b.a, gather_b.b)
    gather_b.step(*gather_a.pieces[:2])
    own_a, oth_a = gather_a.done()

    normed_one, factor_one = normalize(moved[:count].astype(F32))
    qkv, mixed, hat_one, part, away = attend_call(tokens_all, own_a, oth_a, docs, cosine, sine)
    swapped = swap(away)
    gather_b.step(away)
    residual = moved[:count].astype(F32) + part + swapped.astype(F32)
    normed_two, factor_two = normalize(residual)
    hat_own = normed_two.astype(BF)
    gather_b.early(hat_own)
    hat_two = jnp.concatenate([hat_own, swap(hat_own)], axis=0)
    gather_b.step(hat_two)
    own_b, oth_b = gather_b.done()

    three_b, part, away, out_part, out_away = mlp_call(hat_two, cot_all, own_b, oth_b)
    swapped = swap(away)
    side_b = weight_grads(hat_two, cot_all, three_b, None, 1)
    cross_b = ring.across(side_b)
    main_b = weight_grads(tie(hat_two, side_b), cot_all, three_b, None, 0)
    reduce_b = Reduce(ring, main_b, cross_b)
    reduce_b.step()
    grad_hat_two = part + tie(swapped, *reduce_b.sent).astype(F32)
    grad_residual = moved[count:].astype(F32) + norm_back(grad_hat_two, normed_two, factor_two)
    grad_res_own = grad_residual.astype(BF)
    grad_res_all = jnp.concatenate([grad_res_own, swap(grad_res_own)], axis=0)
    reduce_b.step(grad_res_all)
    three_a, part, away = back_call(
        tie(grad_res_all, *reduce_b.sent), qkv, own_a, oth_a, docs, cosine, sine
    )
    reduce_b.step(away)
    swapped = swap(away)
    side_a = weight_grads(tie(hat_one, *reduce_b.sent), grad_res_all, three_a, mixed, 1)
    cross_a = ring.across(side_a)
    main_a = weight_grads(tie(hat_one, side_a), grad_res_all, three_a, mixed, 0)
    reduce_a = Reduce(ring, main_a, cross_a)
    reduce_a.step()
    reduce_b.step(*reduce_a.sent)
    reduce_a.step(*reduce_b.sent)

    grad_hat_one = part + tie(swapped, *reduce_a.sent).astype(F32)
    grad_input = grad_residual + norm_back(grad_hat_one, normed_one, factor_one)
    top = lax.reduce_precision(grad_input, 8, 7)
    middle = lax.reduce_precision(grad_input - top, 8, 7)
    parts = jnp.concatenate([top, middle, grad_input - top - middle], axis=0).astype(BF)
    spread = ein("te,de->td", parts, chosen)
    grad_input = spread[:count] + spread[count : 2 * count] + spread[2 * count :]
    out_swapped = swap(tie(out_away, swapped))
    output = (residual + out_part + tie(out_swapped, *reduce_a.sent).astype(F32)).astype(BF)
    output = ein("te,de->td", output, chosen).astype(BF)
    reduce_a.step(grad_input, output)

    raw_b = reduce_b.done(*reduce_a.sent)
    reduce_a.step(raw_b)
    raw_b = tie(raw_b, *reduce_a.sent)[:, :, :hidden]
    grad_in = jnp.transpose(raw_b[:2] * gain_two[None, :, None], (1, 0, 2))
    grad_mo = raw_b[2].T
    gain_two_sum = jnp.sum(plain_in * raw_b[:2], axis=(0, 2))
    raw_a = reduce_a.done()

    gain_sums = jnp.stack(
        [jnp.sum(plain_qkv * raw_a[:3], axis=(0, 2)), gain_two_sum]
    )
    share = rows // 2
    gain_shares = lax.dynamic_slice_in_dim(gain_sums, side * share, share, 1) + swap(
        lax.dynamic_slice_in_dim(gain_sums, (1 - side) * share, share, 1)
    )
    return (
        output,
        grad_input,
        gain_shares[0],
        jnp.transpose(raw_a[:3] * gain_one[None, :, None], (1, 0, 2)),
        raw_a[3].T,
        gain_shares[1],
        grad_in,
        grad_mo,
    )


def solution(mesh):
    return jax.shard_map(
        body,
        mesh=mesh,
        in_specs=(
            P(("dp", "tensor"), None),
            P("dp", None),
            P("dp"),
            P("dp", None, "tensor"),
            P("tensor", "dp"),
            P("dp"),
            P("dp", None, "tensor"),
            P("tensor", "dp"),
            P(("dp", "tensor"), None),
        ),
        out_specs=(
            P(("dp", "tensor"), None),
            P(("dp", "tensor"), None),
            P(("dp", "tensor")),
            P("dp", None, "tensor"),
            P("tensor", "dp"),
            P(("dp", "tensor")),
            P("dp", None, "tensor"),
            P("tensor", "dp"),
        ),
        check_vma=False,
    )
```
